32 devices in a mesh: grp: 8 (over y, x, core), dir: 4 (over z).
Axes of the slice: x: 2, y: 2, z: 4, core: 2. Of those that a mesh axis runs over, the one named last changes fastest.
Arguments:
- currents: bfloat16 [256, 64, 256], P(('grp', 'dir')), may hold values from -6 to 6
- live_counts: int32 [256], P(('grp', 'dir')), may hold values from 32 to 128, as said below
- radiation: bfloat16 [1024, 2, 128], replicated, may hold values from -0.375 to 0.375
- sources: int32 [256, 189], P('grp'), may hold values from 0 to 255, as said below
- operator_ids: int32 [256, 189], P('grp'), may hold values from 0 to 315
- translators: bfloat16 [316, 2, 1024], P(None, None, 'dir'), may hold values from -0.4375 to 0.4375
- stencil: int32 [1024, 8], P('dir'), may hold values from 0 to 1023, as said below
- stencil_weights: bfloat16 [1024, 8], P('dir'), may hold values from -3 to 3
- receiving: bfloat16 [1024, 2, 128], replicated, may hold values from -0.125 to 0.125
Outputs:
- product: float32 [256, 64, 256], P(('grp', 'dir'))
The draws below stay inside these ranges and needn't reach their ends.
Inputs may be any that keep to these rules, and one draw needn't show every extreme that they name: `live_counts`: some box holds all 128 basis functions. `sources`: every entry lies within 32 of its own box's index, and that distance is reached; entries of a list may repeat. `stencil`: each row names 8 distinct directions within 8 of the row's own direction, counted cyclically over 1024; the distance 8 is reached.
All inputs are finite; a program needn't handle non-finite values.
Results may differ from the reference program's by a relative error of at most 0.0054.
Values may be sent and summed in bfloat16 or wider, within the bound.
No kernel may reach another device: no remote copies, remote signals or barrier semaphores. Data moves between devices by JAX's collectives and lax.ppermute only.
A program may use at most 64 MiB of HBM per device.

```python
import jax
import jax.numpy as jnp
from jax import lax

INCID = 64
UNK = 128
DIRS = 1024
LIST = 189
NOPS = 316
STENCIL = 8
RIM = 8
BOX_DEV = 8
REACH = 32
BOXES = 256
N_GRP = 8
N_DIR = 4


def draw_live_counts(key, part):
    key_counts, key_pick = jax.random.split(jax.random.fold_in(key, 23))
    counts = jax.random.randint(key_counts, (BOXES,), UNK // 4, UNK + 1)
    chosen_box = jax.random.randint(key_pick, (), 0, BOXES)
    box_ids = jnp.arange(BOXES, dtype=jnp.int32)
    return jnp.where(box_ids == chosen_box, UNK, counts).astype(jnp.int32)


def draw_sources(key, part):
    key_offset, key_column, key_sign = jax.random.split(jax.random.fold_in(key, 11), 3)
    centre = jnp.arange(BOXES, dtype=jnp.int32)[:, None]
    offset = jax.random.randint(key_offset, (BOXES, LIST), -REACH, REACH + 1)
    far_column = jax.random.randint(key_column, (BOXES,), 0, LIST)
    sign_pick = jax.random.randint(key_sign, (BOXES,), 0, 2) * 2 - 1
    column = jnp.arange(LIST, dtype=jnp.int32)[None, :]
    offset = jnp.where(column == far_column[:, None], (sign_pick * REACH)[:, None], offset)
    return jnp.clip(centre + offset, 0, BOXES - 1).astype(jnp.int32)


def draw_stencil(key, part):
    key_order, key_side = jax.random.split(jax.random.fold_in(key, 37))
    spread = 2 * RIM + 1
    row_keys = jax.random.split(key_order, DIRS)
    orders = jax.vmap(lambda one_key: jax.random.permutation(one_key, spread))(row_keys)
    side_pick = jax.random.randint(key_side, (DIRS,), 0, 2) * (2 * RIM)
    candidates = jnp.arange(spread, dtype=jnp.int32)
    ranking = jnp.where(candidates[None, :] == side_pick[:, None], -1, orders)
    chosen = jnp.argsort(ranking, axis=1)[:, :STENCIL]
    offsets = chosen - RIM
    own_dirs = jnp.arange(DIRS, dtype=jnp.int32)[:, None]
    return ((own_dirs + offsets) % DIRS).astype(jnp.int32)


def set_ends(drawn, key, low, top_value):
    shape = drawn.shape
    spot = [jax.random.randint(jax.random.fold_in(key, axis), (), 0, shape[axis]) for axis in range(len(shape))]
    drawn = drawn.at[tuple(spot)].set(low)
    longest = shape.index(max(shape))
    spot[longest] = (spot[longest] + 1) % shape[longest]
    return drawn.at[tuple(spot)].set(top_value)


def level_of(stream_key, dims, shards, smallest, high):
    factor_of, own = 1.0, jax.random.fold_in(stream_key, 6)
    for position, blocks in shards:
        heights = jnp.exp(jax.random.uniform(jax.random.fold_in(own, position), (blocks,), jnp.float32, smallest / len(shards), high / len(shards)))
        factor_of = factor_of * jnp.repeat(heights, dims[position] // blocks).reshape([-1 if axis == position else 1 for axis in range(len(dims))])
    return factor_of


def bell_draw(stream_key, extent, scale, bound, cuts=(), kind=jnp.bfloat16):
    gain = level_of(stream_key, extent, cuts, -0.22, 0.18) if cuts else 1.0
    values = jax.random.normal(stream_key, extent, jnp.float32) * scale * gain
    return jnp.minimum(jnp.maximum(values, -bound), bound).astype(kind)


def setup_inputs(seed: int = 0) -> dict:
    arg_keys = jax.random.split(jax.random.key(seed), 10)
    return {
        "currents": bell_draw(arg_keys[0], (BOXES, INCID, 2 * UNK), 1.0, 6.0, ((0, 32),)),
        "live_counts": draw_live_counts(jax.random.fold_in(arg_keys[9], 71), 0),
        "radiation": bell_draw(arg_keys[2], (DIRS, 2, UNK), (2 * UNK) ** -0.5, 0.375),
        "sources": draw_sources(jax.random.fold_in(arg_keys[9], 71), 0),
        "operator_ids": set_ends(jax.random.randint(arg_keys[4], (BOXES, LIST), 0, NOPS), jax.random.fold_in(arg_keys[4], 1), 0, NOPS - 1).astype(jnp.int32),
        "translators": bell_draw(arg_keys[5], (NOPS, 2, DIRS), LIST ** -0.5, 0.4375, ((2, 4),)),
        "stencil": draw_stencil(jax.random.fold_in(arg_keys[9], 71), 0),
        "stencil_weights": bell_draw(arg_keys[7], (DIRS, STENCIL), 0.5, 3.0, ((0, 4),)),
        "receiving": bell_draw(arg_keys[8], (DIRS, 2, UNK), (2 * DIRS) ** -0.5, 0.125),
    }


def mask_rows(values, live_counts):
    column = jnp.arange(values.shape[-1], dtype=jnp.int32) % UNK
    keep = column[None, None, :] < live_counts[:, None, None]
    return jnp.where(keep, values, jnp.zeros_like(values))


def radiation_block(table):
    real_part = table[:, 0, :]
    imag_part = table[:, 1, :]
    upper = jnp.concatenate([real_part, -imag_part], axis=1)
    lower = jnp.concatenate([imag_part, real_part], axis=1)
    return jnp.stack([upper, lower], axis=1)


def receive_block(table):
    real_part = table[:, 0, :]
    imag_part = table[:, 1, :]
    upper = jnp.concatenate([real_part, imag_part], axis=1)
    lower = jnp.concatenate([-imag_part, real_part], axis=1)
    return jnp.stack([upper, lower], axis=1)


def reference(currents, live_counts, radiation, sources, operator_ids, translators, stencil, stencil_weights, receiving):
    box_total = currents.shape[0]
    masked = mask_rows(currents, live_counts)
    forward = radiation_block(radiation).reshape(2 * DIRS, 2 * UNK)
    flattened = masked.reshape(box_total * INCID, 2 * UNK)
    pattern = jnp.dot(forward, flattened.T, preferred_element_type=jnp.float32)
    pattern = pattern.reshape(DIRS, 2, box_total, INCID).transpose(0, 2, 1, 3)
    pattern = pattern.reshape(DIRS, box_total, 2 * INCID).astype(jnp.bfloat16)

    group_boxes = BOX_DEV * N_DIR
    window_width = 3 * group_boxes
    padded = jnp.pad(pattern, ((0, 0), (group_boxes, group_boxes), (0, 0)))

    def one_group(group_id):
        first = group_id * group_boxes
        window = lax.dynamic_slice_in_dim(padded, first, window_width, 1).astype(jnp.float32)
        local_rows = lax.dynamic_slice_in_dim(sources, first, group_boxes, 0) - (first - group_boxes)
        kinds_here = lax.dynamic_slice_in_dim(operator_ids, first, group_boxes, 0)
        picked = translators[kinds_here].astype(jnp.float32)
        box_ids = jnp.broadcast_to(jnp.arange(group_boxes, dtype=jnp.int32)[:, None], local_rows.shape)
        matrix = jnp.zeros((group_boxes, window_width, 2, DIRS), jnp.float32)
        matrix = matrix.at[box_ids, local_rows].add(picked)
        matrix = lax.optimization_barrier(matrix.astype(jnp.bfloat16)).astype(jnp.float32)
        result = jnp.einsum('bsck,ksx->kcbx', matrix, window, precision=lax.Precision.HIGHEST)
        result = result.reshape(DIRS, 2, group_boxes, 2, INCID)
        real_part = result[:, 0, :, 0] - result[:, 1, :, 1]
        imag_part = result[:, 0, :, 1] + result[:, 1, :, 0]
        return jnp.concatenate([real_part, imag_part], axis=-1).astype(jnp.bfloat16)

    translated = lax.map(one_group, jnp.arange(N_GRP, dtype=jnp.int32))
    translated = translated.transpose(1, 0, 2, 3).reshape(DIRS, box_total, 2 * INCID)

    def add_point(total, entry):
        columns, gains = entry
        return total + gains.astype(jnp.float32)[:, None, None] * translated[columns].astype(jnp.float32), None

    filtered, _ = lax.scan(add_point, jnp.zeros((DIRS, box_total, 2 * INCID), jnp.float32), (stencil.T, stencil_weights.T))
    filtered = filtered.astype(jnp.bfloat16)

    backward = receive_block(receiving).reshape(2 * DIRS, 2 * UNK)
    arranged = filtered.reshape(DIRS, box_total, 2, INCID).transpose(1, 3, 0, 2).reshape(box_total * INCID, 2 * DIRS)
    result = jnp.dot(arranged, backward, preferred_element_type=jnp.float32).reshape(box_total, INCID, 2 * UNK)
    return mask_rows(result, live_counts)
```

```python
import functools

import jax
import jax.numpy as jnp
from jax import lax
from jax.experimental import pallas as pl
from jax.experimental.pallas import tpu as pltpu
from jax.sharding import PartitionSpec as P

RIM = 8
LANES = 128
BF = jnp.bfloat16
F32 = jnp.float32
NT = (((1,), (1,)), ((), ()))
TN = (((0,), (0,)), ((), ()))
NN = (((1,), (0,)), ((), ()))
VMEM = pl.BlockSpec(memory_space=pltpu.VMEM)


def round_up(value, unit):
    return -(-value // unit) * unit


def dot(a, b, dims):
    return lax.dot_general(a, b, dims, preferred_element_type=F32)


def cost(flops, nbytes):
    return pl.CostEstimate(flops=int(flops), bytes_accessed=int(nbytes), transcendentals=0)


def tables_kernel(
    src_ref, op_ref, table_ref, offset_ref, weight_ref, receive_ref, matrix_ref, folded_ref, wide
):
    boxes, width = src_ref.shape
    dirs, rows, window = matrix_ref.shape
    kinds = table_ref.shape[1]

    def one_box(box, carry):
        src = src_ref[pl.ds(box, 1), :]
        ops = op_ref[pl.ds(box, 1), :]
        hit_kind = (lax.broadcasted_iota(jnp.int32, (kinds, width), 0) == ops).astype(F32).astype(BF)
        hit_src = (lax.broadcasted_iota(jnp.int32, (window, width), 0) == src).astype(F32).astype(BF)
        counts = dot(hit_kind, hit_src, NT).astype(BF)
        entries = dot(table_ref[...], counts, NN)
        for c in range(window // LANES):
            part = entries[:, c * LANES : (c + 1) * LANES]
            wide[c, pl.ds(box, dirs, stride=rows), :] = part[:dirs]
            wide[c, pl.ds(box + boxes, dirs, stride=rows), :] = part[dirs:]
        return carry

    lax.fori_loop(0, boxes, one_box, 0)

    def narrow(step, carry):
        for i in range(4):
            k = step * 4 + i
            for c in range(window // LANES):
                part = wide[c, pl.ds(pl.multiple_of(k * rows, 8), rows), :]
                matrix_ref[k, :, c * LANES : (c + 1) * LANES] = part.astype(BF)
        return carry

    lax.fori_loop(0, dirs // 4, narrow, 0)

    extent = offset_ref.shape[1]
    own = lax.broadcasted_iota(jnp.int32, (dirs, extent), 0)
    spread = jnp.zeros((dirs, extent), F32)
    for p in range(offset_ref.shape[0]):
        spread += jnp.where(own == offset_ref[p : p + 1, :], weight_ref[p : p + 1, :], 0.0)
    folded_ref[...] = dot(spread.astype(BF), receive_ref[...], NN).astype(BF)


def build_tables(src, ops, table, offsets, weights, receive, dirs, window):
    boxes = src.shape[0]
    return pl.pallas_call(
        tables_kernel,
        out_shape=(
            jax.ShapeDtypeStruct((dirs, 2 * boxes, window), BF),
            jax.ShapeDtypeStruct((dirs, receive.shape[1]), BF),
        ),
        in_specs=[VMEM] * 6,
        out_specs=(VMEM, VMEM),
        scratch_shapes=[pltpu.VMEM((window // LANES, dirs * 2 * boxes, LANES), F32)],
        cost_estimate=cost(2 * boxes * 2 * dirs * 320 * window * 4, 8 << 20),
        name="tables",
    )(src, ops, table, offsets, weights, receive)


def rotated(box):
    half = box.shape[1] // 2
    re, im = box[:, :half], box[:, half:]
    return jnp.concatenate(
        [jnp.concatenate([re, -im], axis=1), jnp.concatenate([im, re], axis=1)], axis=0
    )


def radiate(forward_ref, box_refs, out, stride):
    dirs = forward_ref.shape[0]
    first = 0
    for ref in box_refs:
        count = ref.shape[0]
        width = 2 * ref.shape[1]

        def pair(step, carry, ref=ref, first=first, width=width):
            both = jnp.concatenate([rotated(ref[2 * step]), rotated(ref[2 * step + 1])], axis=0)
            field = dot(forward_ref[...], both, NT)
            at = first + 2 * step
            out[pl.ds(at, dirs, stride=stride), :] = field[:, :width]
            out[pl.ds(at + 1, dirs, stride=stride), :] = field[:, width:]
            return carry

        lax.fori_loop(0, count // 2, pair, 0)
        first += count


def pattern_kernel(count, forward_ref, *refs):
    box_refs, pattern_ref, wide = refs[:count], refs[count], refs[count + 1]
    dirs, boxes, _ = pattern_ref.shape
    radiate(forward_ref, box_refs, wide, boxes)

    def narrow(step, carry):
        for i in range(4):
            k = step * 4 + i
            pattern_ref[k] = wide[pl.ds(pl.multiple_of(k * boxes, 8), boxes), :].astype(BF)
        return carry

    lax.fori_loop(0, dirs // 4, narrow, 0)


def own_pattern(forward, shards):
    dirs = forward.shape[0]
    boxes = sum(s.shape[0] for s in shards)
    width = 2 * shards[0].shape[1]
    return pl.pallas_call(
        functools.partial(pattern_kernel, len(shards)),
        out_shape=jax.ShapeDtypeStruct((dirs, boxes, width), BF),
        in_specs=[VMEM] * (1 + len(shards)),
        out_specs=VMEM,
        scratch_shapes=[pltpu.VMEM((dirs * boxes, width), F32)],
        cost_estimate=cost(2 * dirs * boxes * width * 256, 4 << 20),
        name="pattern",
    )(forward, *shards)


def field_kernel(count, forward_ref, matrix_ref, folded_ref, own_ref, *refs):
    box_refs = refs[: 2 * count]
    out_refs = refs[2 * count : 3 * count]
    near, moved = refs[3 * count :]
    dirs, own_boxes, width = own_ref.shape
    near_boxes = 2 * own_boxes
    boxes = matrix_ref.shape[1] // 2
    half = width // 2
    radiate(forward_ref, box_refs, near, near_boxes)
    lane = lax.broadcasted_iota(jnp.int32, (boxes, width), 1)
    sign = jnp.where(lane < half, -1.0, 1.0).astype(F32)

    def translate(step, carry):
        for i in range(4):
            k = step * 4 + i
            around = near[pl.ds(pl.multiple_of(k * near_boxes, 8), near_boxes), :].astype(BF)
            fields = jnp.concatenate([own_ref[k], around], axis=0)
            both = dot(matrix_ref[k][:, : own_boxes + near_boxes], fields, NN)
            turned = pltpu.roll(both[boxes:], half, 1)
            moved[pl.ds(pl.multiple_of(k * boxes, 8), boxes), :] = both[:boxes] + sign * turned
        return carry

    lax.fori_loop(0, dirs // 4, translate, 0)

    per = boxes // count
    unk = folded_ref.shape[1] // 2
    for j, out_ref in enumerate(out_refs):

        def receive(i, carry, j=j, out_ref=out_ref):
            field = moved[pl.ds(j * per + i, dirs, stride=boxes), :].astype(BF)
            full = dot(field, folded_ref[...], TN)
            re = full[:half, :unk] - full[half:, unk:]
            im = full[:half, unk:] + full[half:, :unk]
            out_ref[i] = jnp.concatenate([re, im], axis=1).astype(out_ref.dtype)
            return carry

        lax.fori_loop(0, per, receive, 0)


def receive_field(forward, matrix, folded, own, left, right):
    count = len(left)
    dirs, own_boxes, width = own.shape
    per = matrix.shape[1] // 2 // count
    kinds = [F32] + [BF] * (count - 1)
    return pl.pallas_call(
        functools.partial(field_kernel, count),
        out_shape=tuple(
            jax.ShapeDtypeStruct((per, width // 2, folded.shape[1]), kind) for kind in kinds
        ),
        in_specs=[VMEM] * (4 + 2 * count),
        out_specs=(VMEM,) * count,
        scratch_shapes=[
            pltpu.VMEM((dirs * 2 * own_boxes, width), F32),
            pltpu.VMEM((dirs * matrix.shape[1] // 2, width), F32),
        ],
        cost_estimate=cost(4 << 30, 16 << 20),
        name="field",
    )(forward, matrix, folded, own, *left, *right)


def mask_rows(values, live_counts):
    column = jnp.arange(values.shape[-1], dtype=jnp.int32) % (values.shape[-1] // 2)
    keep = column[None, None, :] < live_counts[:, None, None]
    return jnp.where(keep, values, jnp.zeros_like(values))


def body(
    currents,
    live_counts,
    radiation,
    sources,
    operator_ids,
    translators,
    stencil,
    stencil_weights,
    receiving,
):
    dir_index = lax.axis_index("dir")
    n_dir, n_grp = lax.axis_size("dir"), lax.axis_size("grp")
    kinds, _, dirs = translators.shape
    all_dirs = radiation.shape[0]
    per = currents.shape[0]
    boxes = n_dir * per
    window = round_up(3 * boxes, 128)

    def turn(values, step):
        return lax.ppermute(values, "dir", [(i, (i + step) % n_dir) for i in range(n_dir)])

    def shift(values, step):
        pairs = [(i, i + step) for i in range(n_grp) if 0 <= i + step < n_grp]
        return lax.ppermute(values, "grp", pairs)

    masked = mask_rows(currents, live_counts)
    shards = [masked] + [turn(masked, j) for j in range(1, n_dir)]
    left = [shift(s, 1) for s in shards]
    right = [shift(s, -1) for s in shards]

    local = sources - (lax.axis_index("grp") - 1) * boxes
    group, inside = local // boxes, local % boxes
    slot = (dir_index - inside // per) % n_dir
    place = jnp.where(group == 1, 0, jnp.where(group == 0, 1, 2))
    place = place * boxes + slot * per + inside % per
    pad = round_up(sources.shape[1], 128) - sources.shape[1]
    lists = jnp.stack([place, operator_ids])
    lists = jnp.pad(lists, ((0, 0), (0, 0), (0, pad)), constant_values=-1)
    lists = lax.dynamic_slice_in_dim(
        jnp.concatenate([lists, lists], axis=1), dir_index * per, boxes, 1
    )
    table = translators.transpose(1, 2, 0).reshape(2 * dirs, kinds)
    table = jnp.pad(table, ((0, 0), (0, round_up(kinds, 64) - kinds)))

    own_dirs = dir_index * dirs + jnp.arange(dirs, dtype=jnp.int32)
    distance = (stencil - own_dirs[:, None]) % all_dirs
    distance = jnp.where(distance > all_dirs // 2, distance - all_dirs, distance)
    rows = jnp.concatenate([distance.astype(BF), stencil_weights], axis=1)
    rows = jnp.concatenate([turn(rows[-RIM:], 1), rows, turn(rows[:RIM], -1)], axis=0)
    extent = dirs + 2 * RIM
    fill = round_up(extent, 128) - extent
    points = stencil.shape[1]
    position = jnp.arange(extent, dtype=jnp.int32)[:, None] - RIM
    offsets = jnp.pad((position + rows[:, :points].astype(jnp.int32)).T, ((0, 0), (0, fill)))
    weights = jnp.pad(rows[:, points:].astype(F32).T, ((0, 0), (0, fill)))
    flat = receiving.reshape(all_dirs, -1)
    around = jnp.concatenate([flat[-RIM:], flat, flat[: RIM + fill]], axis=0)
    receive = lax.dynamic_slice_in_dim(around, dir_index * dirs, extent + fill, 0)
    forward = lax.dynamic_slice_in_dim(
        radiation.reshape(all_dirs, -1), dir_index * dirs, dirs, 0
    )

    matrix, folded = build_tables(
        lists[0], lists[1], table, offsets, weights, receive, dirs, window
    )
    own = own_pattern(forward, shards)
    parts = receive_field(forward, matrix, folded, own, left, right)
    total = parts[0]
    for j in range(1, n_dir):
        total = total + turn(parts[j], j).astype(F32)
    return mask_rows(total, live_counts)


def solution(mesh):
    placed = (
        P(("grp", "dir"), None, None),
        P(("grp", "dir")),
        P(),
        P("grp", None),
        P("grp", None),
        P(None, None, "dir"),
        P("dir", None),
        P("dir", None),
        P(),
    )
    return jax.shard_map(
        body, mesh=mesh, in_specs=placed, out_specs=P(("grp", "dir"), None, None), check_vma=False
    )
```

```python
import functools

import jax
import jax.numpy as jnp
from jax import lax
from jax.experimental import pallas as pl
from jax.experimental.pallas import tpu as pltpu
from jax.sharding import PartitionSpec as P

RIM = 8
LANES = 128
BF = jnp.bfloat16
F32 = jnp.float32
NT = (((1,), (1,)), ((), ()))
TN = (((0,), (0,)), ((), ()))
NN = (((1,), (0,)), ((), ()))
VMEM = pl.BlockSpec(memory_space=pltpu.VMEM)


def round_up(value, unit):
    return -(-value // unit) * unit


def dot(a, b, dims):
    return lax.dot_general(a, b, dims, preferred_element_type=F32)


def cost(flops, nbytes):
    return pl.CostEstimate(flops=int(flops), bytes_accessed=int(nbytes), transcendentals=0)


def unrolled(trips, most, step):
    size = next(n for n in range(min(most, trips), 0, -1) if trips % n == 0)

    def block(i, carry):
        for j in range(size):
            step(i * size + j)
        return carry

    lax.fori_loop(0, trips // size, block, 0)


def tables_kernel(
    src_ref, op_ref, table_ref, offset_ref, weight_ref, receive_ref, matrix_ref, folded_ref, wide
):
    boxes, width = src_ref.shape
    dirs, rows, window = matrix_ref.shape
    kinds = table_ref.shape[1]

    def two_boxes(step):
        counts = []
        for box in (2 * step, 2 * step + 1):
            src = src_ref[pl.ds(box, 1), :]
            ops = op_ref[pl.ds(box, 1), :]
            hit_kind = lax.broadcasted_iota(jnp.int32, (kinds, width), 0) == ops
            hit_src = lax.broadcasted_iota(jnp.int32, (window, width), 0) == src
            counts.append(dot(hit_kind.astype(F32).astype(BF), hit_src.astype(F32).astype(BF), NT))
        counts = jnp.concatenate(counts, axis=1).astype(BF)
        entries = dot(table_ref[...], counts, NN)
        for i in range(2):
            for c in range(window // LANES):
                part = entries[:, i * window + c * LANES : i * window + (c + 1) * LANES]
                at = 2 * step + i
                wide[c, pl.ds(at, dirs, stride=rows + 1), :] = part[:dirs]
                wide[c, pl.ds(at + boxes, dirs, stride=rows + 1), :] = part[dirs:]

    unrolled(boxes // 2, 2, two_boxes)

    def narrow(k):
        for c in range(window // LANES):
            part = wide[c, pl.ds(k * (rows + 1), rows), :]
            matrix_ref[k, :, c * LANES : (c + 1) * LANES] = part.astype(BF)

    unrolled(dirs, 8, narrow)

    extent = offset_ref.shape[1]
    own = lax.broadcasted_iota(jnp.int32, (dirs, extent), 0)
    spread = jnp.zeros((dirs, extent), F32)
    for p in range(offset_ref.shape[0]):
        spread += jnp.where(own == offset_ref[p : p + 1, :], weight_ref[p : p + 1, :], 0.0)
    folded_ref[...] = dot(spread.astype(BF), receive_ref[...], NN).astype(BF)


def build_tables(src, ops, table, offsets, weights, receive, dirs, window):
    boxes = src.shape[0]
    return pl.pallas_call(
        tables_kernel,
        out_shape=(
            jax.ShapeDtypeStruct((dirs, 2 * boxes, window), BF),
            jax.ShapeDtypeStruct((dirs, receive.shape[1]), BF),
        ),
        in_specs=[VMEM] * 6,
        out_specs=(VMEM, VMEM),
        scratch_shapes=[pltpu.VMEM((window // LANES, dirs * (2 * boxes + 1), LANES), F32)],
        cost_estimate=cost(2 * boxes * 2 * dirs * 320 * window * 4, 8 << 20),
        name="tables",
    )(src, ops, table, offsets, weights, receive)


def rotated(box):
    half = box.shape[1] // 2
    re, im = box[:, :half], box[:, half:]
    return jnp.concatenate(
        [jnp.concatenate([re, -im], axis=1), jnp.concatenate([im, re], axis=1)], axis=0
    )


def radiate(forward_ref, box_refs, out, stride):
    dirs = forward_ref.shape[0]
    first = 0
    for ref in box_refs:
        width = 2 * ref.shape[1]

        def pair(step, ref=ref, first=first, width=width):
            both = jnp.concatenate([rotated(ref[2 * step]), rotated(ref[2 * step + 1])], axis=0)
            field = dot(forward_ref[...], both, NT)
            at = first + 2 * step
            out[pl.ds(at, dirs, stride=stride), :] = field[:, :width]
            out[pl.ds(at + 1, dirs, stride=stride), :] = field[:, width:]

        for step in range(ref.shape[0] // 2):
            pair(step)
        first += ref.shape[0]


def pattern_kernel(count, forward_ref, *refs):
    box_refs, pattern_ref, wide = refs[:count], refs[count], refs[count + 1]
    dirs, boxes, _ = pattern_ref.shape
    radiate(forward_ref, box_refs, wide, boxes + 1)

    def narrow(k):
        pattern_ref[k] = wide[pl.ds(k * (boxes + 1), boxes), :].astype(BF)

    unrolled(dirs, 16, narrow)


def own_pattern(forward, shards):
    dirs = forward.shape[0]
    boxes = sum(s.shape[0] for s in shards)
    width = 2 * shards[0].shape[1]
    return pl.pallas_call(
        functools.partial(pattern_kernel, len(shards)),
        out_shape=jax.ShapeDtypeStruct((dirs, boxes, width), BF),
        in_specs=[VMEM] * (1 + len(shards)),
        out_specs=VMEM,
        scratch_shapes=[pltpu.VMEM((dirs * (boxes + 1), width), F32)],
        cost_estimate=cost(2 * dirs * boxes * width * 256, 4 << 20),
        name="pattern",
    )(forward, *shards)


def field_kernel(count, forward_ref, matrix_ref, folded_ref, own_ref, *refs):
    box_refs = refs[: 2 * count]
    out_refs = refs[2 * count : 3 * count]
    near, moved = refs[3 * count :]
    dirs, own_boxes, width = own_ref.shape
    near_boxes = 2 * own_boxes
    boxes = matrix_ref.shape[1] // 2
    half = width // 2
    radiate(forward_ref, box_refs, near, near_boxes + 1)
    lane = lax.broadcasted_iota(jnp.int32, (boxes, width), 1)
    sign = jnp.where(lane < half, -1.0, 1.0).astype(F32)

    def translate(k):
        around = near[pl.ds(k * (near_boxes + 1), near_boxes), :].astype(BF)
        fields = jnp.concatenate([own_ref[k], around], axis=0)
        both = dot(matrix_ref[k][:, : own_boxes + near_boxes], fields, NN)
        turned = pltpu.roll(both[boxes:], half, 1)
        moved[pl.ds(k * (boxes + 1), boxes), :] = both[:boxes] + sign * turned

    unrolled(dirs, 64 * 32 // boxes, translate)

    per = boxes // count
    unk = folded_ref.shape[1] // 2
    for j, out_ref in enumerate(out_refs):
        for i in range(per):
            field = moved[pl.ds(j * per + i, dirs, stride=boxes + 1), :].astype(BF)
            full = dot(field, folded_ref[...], TN)
            re = full[:half, :unk] - full[half:, unk:]
            im = full[:half, unk:] + full[half:, :unk]
            out_ref[i] = jnp.concatenate([re, im], axis=1).astype(out_ref.dtype)


def receive_field(forward, matrix, folded, own, left, right):
    count = len(left)
    dirs, own_boxes, width = own.shape
    per = matrix.shape[1] // 2 // count
    kinds = [F32] + [BF] * (count - 1)
    return pl.pallas_call(
        functools.partial(field_kernel, count),
        out_shape=tuple(
            jax.ShapeDtypeStruct((per, width // 2, folded.shape[1]), kind) for kind in kinds
        ),
        in_specs=[VMEM] * (4 + 2 * count),
        out_specs=(VMEM,) * count,
        scratch_shapes=[
            pltpu.VMEM((dirs * (2 * own_boxes + 1), width), F32),
            pltpu.VMEM((dirs * (matrix.shape[1] // 2 + 1), width), F32),
        ],
        cost_estimate=cost(4 << 30, 16 << 20),
        name="field",
    )(forward, matrix, folded, own, *left, *right)


def mask_rows(values, live_counts):
    column = jnp.arange(values.shape[-1], dtype=jnp.int32) % (values.shape[-1] // 2)
    keep = column[None, None, :] < live_counts[:, None, None]
    return jnp.where(keep, values, jnp.zeros_like(values))


def body(
    currents,
    live_counts,
    radiation,
    sources,
    operator_ids,
    translators,
    stencil,
    stencil_weights,
    receiving,
):
    dir_index = lax.axis_index("dir")
    n_dir, n_grp = lax.axis_size("dir"), lax.axis_size("grp")
    kinds, _, dirs = translators.shape
    all_dirs = radiation.shape[0]
    per = currents.shape[0]
    boxes = n_dir * per
    window = round_up(3 * boxes, 128)

    def turn(values, step):
        return lax.ppermute(values, "dir", [(i, (i + step) % n_dir) for i in range(n_dir)])

    def shift(values, step):
        pairs = [(i, i + step) for i in range(n_grp) if 0 <= i + step < n_grp]
        return lax.ppermute(values, "grp", pairs)

    masked = mask_rows(currents, live_counts)
    shards = [masked] + [turn(masked, j) for j in range(1, n_dir)]
    left = [shift(s, 1) for s in shards]
    right = [shift(s, -1) for s in shards]

    local = sources - (lax.axis_index("grp") - 1) * boxes
    group, inside = local // boxes, local % boxes
    slot = (dir_index - inside // per) % n_dir
    place = jnp.where(group == 1, 0, jnp.where(group == 0, 1, 2))
    place = place * boxes + slot * per + inside % per
    pad = round_up(sources.shape[1], 128) - sources.shape[1]
    lists = jnp.stack([place, operator_ids])
    lists = jnp.pad(lists, ((0, 0), (0, 0), (0, pad)), constant_values=-1)
    lists = lax.dynamic_slice_in_dim(
        jnp.concatenate([lists, lists], axis=1), dir_index * per, boxes, 1
    )
    table = translators.transpose(1, 2, 0).reshape(2 * dirs, kinds)
    table = jnp.pad(table, ((0, 0), (0, round_up(kinds, LANES) - kinds)))

    own_dirs = dir_index * dirs + jnp.arange(dirs, dtype=jnp.int32)
    distance = (stencil - own_dirs[:, None]) % all_dirs
    distance = jnp.where(distance > all_dirs // 2, distance - all_dirs, distance)
    rows = jnp.concatenate([distance.astype(BF), stencil_weights], axis=1)
    rows = jnp.concatenate([turn(rows[-RIM:], 1), rows, turn(rows[:RIM], -1)], axis=0)
    extent = dirs + 2 * RIM
    fill = round_up(extent, 128) - extent
    points = stencil.shape[1]
    position = jnp.arange(extent, dtype=jnp.int32)[:, None] - RIM
    offsets = jnp.pad((position + rows[:, :points].astype(jnp.int32)).T, ((0, 0), (0, fill)))
    weights = jnp.pad(rows[:, points:].astype(F32).T, ((0, 0), (0, fill)))
    flat = receiving.reshape(all_dirs, -1)
    around = jnp.concatenate([flat[-RIM:], flat, flat[: RIM + fill]], axis=0)
    receive = lax.dynamic_slice_in_dim(around, dir_index * dirs, extent + fill, 0)
    forward = lax.dynamic_slice_in_dim(
        radiation.reshape(all_dirs, -1), dir_index * dirs, dirs, 0
    )

    matrix, folded = build_tables(
        lists[0], lists[1], table, offsets, weights, receive, dirs, window
    )
    own = own_pattern(forward, shards)
    parts = receive_field(forward, matrix, folded, own, left, right)
    total = parts[0]
    for j in range(1, n_dir):
        total = total + turn(parts[j], j).astype(F32)
    return mask_rows(total, live_counts)


def solution(mesh):
    placed = (
        P(("grp", "dir"), None, None),
        P(("grp", "dir")),
        P(),
        P("grp", None),
        P("grp", None),
        P(None, None, "dir"),
        P("dir", None),
        P("dir", None),
        P(),
    )
    return jax.shard_map(
        body, mesh=mesh, in_specs=placed, out_specs=P(("grp", "dir"), None, None), check_vma=False
    )
```

```python
import functools

import jax
import jax.numpy as jnp
from jax import lax
from jax.experimental import pallas as pl
from jax.experimental.pallas import tpu as pltpu
from jax.sharding import PartitionSpec as P

RIM = 8
LANES = 128
BF = jnp.bfloat16
F32 = jnp.float32
I32 = jnp.int32
NT = (((1,), (1,)), ((), ()))
TN = (((0,), (0,)), ((), ()))
NN = (((1,), (0,)), ((), ()))
VMEM = pl.BlockSpec(memory_space=pltpu.VMEM)
SMEM = pl.BlockSpec(memory_space=pltpu.SMEM)


def round_up(value, unit):
    return -(-value // unit) * unit


def dot(a, b, dims):
    return lax.dot_general(a, b, dims, preferred_element_type=F32)


def cost(flops, nbytes):
    return pl.CostEstimate(flops=int(flops), bytes_accessed=int(nbytes), transcendentals=0)


def count_of(shape, axis):
    return lax.broadcasted_iota(I32, shape, axis)


def as_bf16(mask):
    return mask.astype(F32).astype(BF)


def unrolled(trips, most, step):
    size = next(n for n in range(min(most, trips), 0, -1) if trips % n == 0)

    def block(i, carry):
        for j in range(size):
            step(i * size + j)
        return carry

    lax.fori_loop(0, trips // size, block, 0)


def prepare_kernel(rim, all_dirs, place_ref, live_ref, stencil_ref, weight_ref, box_ref, out_ref, point_ref):
    boxes, incid, width = box_ref.shape
    points, dirs = stencil_ref.shape
    unk = count_of((incid, width), 1)
    unk = jnp.where(unk < width // 2, unk, unk - width // 2)
    for b in range(boxes):
        kept = jnp.where(unk < live_ref[b], box_ref[b].astype(F32), 0.0)
        out_ref[b * incid : (b + 1) * incid, :] = kept.astype(BF)
    away = stencil_ref[...] - (count_of((points, dirs), 1) + place_ref[0] * dirs)
    away = jnp.where(away > all_dirs // 2, away - all_dirs, away)
    away = jnp.where(away < -(all_dirs // 2), away + all_dirs, away)
    rows = jnp.concatenate([away.astype(F32), weight_ref[...].astype(F32)], axis=0)
    point_ref[...] = rows
    source, target = count_of((dirs, width), 0), count_of((dirs, width), 1)
    head = (target < rim) & (source == target)
    tail = (target >= rim) & (target < 2 * rim) & (source == target + dirs - 2 * rim)
    out_ref[boxes * incid :, :] = dot(rows.astype(BF), as_bf16(head | tail), NN).astype(BF)


def prepare(place, live_counts, stencil, weights, currents, all_dirs):
    boxes, incid, width = currents.shape
    points, dirs = stencil.shape
    return pl.pallas_call(
        functools.partial(prepare_kernel, RIM, all_dirs),
        out_shape=(
            jax.ShapeDtypeStruct((boxes * incid + 2 * points, width), BF),
            jax.ShapeDtypeStruct((2 * points, dirs), F32),
        ),
        in_specs=[SMEM, SMEM, VMEM, VMEM, VMEM],
        out_specs=(VMEM, VMEM),
        cost_estimate=cost(1 << 20, 1 << 20),
        name="prepare",
    )(place, live_counts, stencil, weights, currents)


def transfer_kernel(first, per, slots, place_ref, source_ref, kind_ref, table_ref, matrix_ref, lists, table, wide):
    all_boxes, width = source_ref.shape
    dirs, rows, window = matrix_ref.shape
    boxes = rows // 2
    kinds = table_ref.shape[0]
    padded = table.shape[1]
    own_dir, own_group = place_ref[0], place_ref[1]

    local = source_ref[...] - (own_group - 1) * all_boxes
    group = (local >= all_boxes).astype(I32) + (local >= 2 * all_boxes).astype(I32)
    inside = local - group * all_boxes
    holder = jnp.zeros_like(inside)
    for j in range(1, slots):
        holder += (inside >= j * per).astype(I32)
    paired = jnp.where(own_group % 2 == 0, 2, 0)
    turn = jnp.where(group == 1, 0, jnp.where(group == paired, 2, 1))
    spot = turn * all_boxes + (own_dir ^ holder) * per + inside - holder * per
    lists[...] = jnp.full(lists.shape, -1, I32)
    lists[:all_boxes, :width] = spot
    lists[all_boxes:, :width] = kind_ref[...]

    fill = jnp.zeros((padded - kinds, dirs), BF)
    for c in range(2):
        part = jnp.concatenate([table_ref[:, c, :], fill], axis=0)
        table[c * dirs : (c + 1) * dirs, :] = part.T

    lanes = lists.shape[1]

    def two_boxes(step):
        counts = []
        for i in range(2):
            at = first + 2 * step + i
            row = (own_dir ^ (at // per)) * per + at % per
            hit_kind = count_of((padded, lanes), 0) == lists[pl.ds(all_boxes + row, 1), :]
            hit_source = count_of((window, lanes), 0) == lists[pl.ds(row, 1), :]
            counts.append(dot(as_bf16(hit_kind), as_bf16(hit_source), NT))
        counts = jnp.concatenate(counts, axis=1).astype(BF)
        entries = dot(table[...], counts, NN)
        for i in range(2):
            for c in range(window // LANES):
                part = entries[:, i * window + c * LANES : i * window + (c + 1) * LANES]
                at = 2 * step + i
                wide[c, pl.ds(at, dirs, stride=rows + 1), :] = part[:dirs]
                wide[c, pl.ds(at + boxes, dirs, stride=rows + 1), :] = part[dirs:]

    unrolled(boxes // 2, 4, two_boxes)

    def narrow(k):
        for c in range(window // LANES):
            part = wide[c, pl.ds(k * (rows + 1), rows), :]
            matrix_ref[k, :, c * LANES : (c + 1) * LANES] = part.astype(BF)

    unrolled(dirs, 16, narrow)


def transfer(place, sources, operator_ids, translators, first, boxes, per, window):
    kinds, _, dirs = translators.shape
    all_boxes, width = sources.shape
    padded = round_up(kinds, LANES)
    return pl.pallas_call(
        functools.partial(transfer_kernel, first, per, all_boxes // per),
        out_shape=jax.ShapeDtypeStruct((dirs, 2 * boxes, window), BF),
        in_specs=[SMEM, VMEM, VMEM, VMEM],
        out_specs=VMEM,
        scratch_shapes=[
            pltpu.VMEM((2 * all_boxes, round_up(width, LANES)), I32),
            pltpu.VMEM((2 * dirs, padded), BF),
            pltpu.VMEM((window // LANES, dirs * (2 * boxes + 1), LANES), F32),
        ],
        cost_estimate=cost(8 << 30, 4 << 20),
        name="transfer",
    )(place, sources, operator_ids, translators)


def rotated(box):
    half = box.shape[1] // 2
    re, im = box[:, :half], box[:, half:]
    return jnp.concatenate(
        [jnp.concatenate([re, -im], axis=1), jnp.concatenate([im, re], axis=1)], axis=0
    )


def radiate(forward, box_refs, incid, out, stride):
    dirs = forward.shape[0]
    at = 0
    for ref in box_refs:
        for row in range(0, ref.shape[0] // incid * incid, 2 * incid):
            both = [rotated(ref[i : i + incid, :]) for i in (row, row + incid)]
            field = dot(forward[...], jnp.concatenate(both, axis=0), NT)
            out[pl.ds(at, dirs, stride=stride), :] = field[:, : 2 * incid]
            out[pl.ds(at + 1, dirs, stride=stride), :] = field[:, 2 * incid :]
            at += 2


def pattern_kernel(
    count, incid, rim, place_ref, forward_ref, receive_ref, after_ref, before_ref, point_ref, *refs
):
    box_refs, (pattern_ref, turned_ref, folded_ref, wide) = refs[:count], refs[count:]
    dirs, boxes, _ = pattern_ref.shape
    turned_ref[...] = jnp.concatenate([forward_ref[:, 0, :], forward_ref[:, 1, :]], axis=1)
    radiate(turned_ref, box_refs, incid, wide, boxes + 1)

    def narrow(k):
        pattern_ref[k] = wide[pl.ds(k * (boxes + 1), boxes), :].astype(BF)

    unrolled(dirs, 16, narrow)

    own_dir = place_ref[0]
    points = point_ref.shape[0] // 2
    lane = count_of((2 * points, LANES), 1)
    ends = jnp.zeros((2 * points, LANES), F32)
    for j, ref in enumerate(box_refs):
        tail = ref[ref.shape[0] - 2 * points :, :LANES].astype(F32)
        holder = own_dir ^ j
        follows = holder == lax.rem(own_dir + 1, count)
        leads = holder == lax.rem(own_dir + count - 1, count)
        here = ((lane < rim) & follows) | ((lane >= rim) & (lane < 2 * rim) & leads)
        ends = jnp.where(here, tail, ends)
    spot = count_of((points, LANES), 1)
    spot = jnp.where(spot < rim, spot + dirs, spot - 2 * rim)
    spots = [point_ref[:points, :].astype(I32) + count_of((points, dirs), 1)]
    spots.append(ends[:points].astype(I32) + spot)
    gains = [point_ref[points:, :], ends[points:]]
    tables = [receive_ref[...], jnp.concatenate([after_ref[...], before_ref[...]], axis=0)]
    folded = None
    for spot, gain, table in zip(spots, gains, tables):
        extent = spot.shape[1]
        own = count_of((dirs, extent), 0)
        spread = jnp.zeros((dirs, extent), F32)
        for p in range(points):
            spread += jnp.where(own == spot[p : p + 1, :], gain[p : p + 1, :], 0.0)
        flat = jnp.concatenate([table[:, 0, :], table[:, 1, :]], axis=1)
        if flat.shape[0] < extent:
            blank = jnp.zeros((extent - flat.shape[0], flat.shape[1]), BF)
            flat = jnp.concatenate([flat, blank], axis=0)
        part = dot(spread.astype(BF), flat, NN)
        folded = part if folded is None else folded + part
    folded_ref[...] = folded.astype(BF)


def own_pattern(place, radiation, receiving, rows, shards, incid, dirs):
    count = len(shards)
    boxes = sum(s.shape[0] // incid for s in shards)
    all_dirs, parts, unk = receiving.shape
    own = pl.BlockSpec((dirs, parts, unk), lambda i, at: (at[0], 0, 0))
    rims, total = dirs // RIM, all_dirs // RIM
    after = pl.BlockSpec((RIM, parts, unk), lambda i, at: (lax.rem((at[0] + 1) * rims, total), 0, 0))
    before = pl.BlockSpec(
        (RIM, parts, unk), lambda i, at: (lax.rem(at[0] * rims + total - 1, total), 0, 0)
    )
    return pl.pallas_call(
        functools.partial(pattern_kernel, count, incid, RIM),
        out_shape=(
            jax.ShapeDtypeStruct((dirs, boxes, 2 * incid), BF),
            jax.ShapeDtypeStruct((dirs, parts * unk), BF),
            jax.ShapeDtypeStruct((dirs, parts * unk), BF),
        ),
        grid_spec=pltpu.PrefetchScalarGridSpec(
            num_scalar_prefetch=1,
            grid=(1,),
            in_specs=[own, own, after, before] + [VMEM] * (1 + count),
            out_specs=(VMEM, VMEM, VMEM),
            scratch_shapes=[pltpu.VMEM((dirs * (boxes + 1), 2 * incid), F32)],
        ),
        cost_estimate=cost(1 << 30, 4 << 20),
        name="pattern",
    )(place, radiation, receiving, receiving, receiving, rows, *shards)


def field_kernel(count, halves, forward_ref, folded_ref, own_ref, *refs):
    matrix_refs, refs = refs[:halves], refs[halves:]
    box_refs, out_refs, (near, moved) = refs[: -count - 2], refs[-count - 2 : -2], refs[-2:]
    dirs, own_boxes, width = own_ref.shape
    near_boxes = 2 * own_boxes
    boxes = matrix_refs[0].shape[1] // 2
    half = width // 2
    radiate(forward_ref, box_refs, half, near, near_boxes + 1)
    sign = jnp.where(count_of((boxes, width), 1) < half, -1.0, 1.0).astype(F32)
    stride = own_boxes + 1

    def translate(k):
        around = near[pl.ds(k * (near_boxes + 1), near_boxes), :].astype(BF)
        fields = jnp.concatenate([own_ref[k], around], axis=0)
        weights = [ref[k][:, : own_boxes + near_boxes] for ref in matrix_refs]
        both = dot(jnp.concatenate(weights, axis=0), fields, NN)
        for h in range(halves):
            part = both[2 * boxes * h : 2 * boxes * (h + 1)]
            turned = pltpu.roll(part[boxes:], half, 1)
            moved[pl.ds(k * stride + h * boxes, boxes), :] = part[:boxes] + sign * turned

    unrolled(dirs, 64 * 32 // own_boxes, translate)

    unk = folded_ref.shape[1] // 2
    per = own_boxes // count
    for j, out_ref in enumerate(out_refs):
        for i in range(per):
            field = moved[pl.ds(j * per + i, dirs, stride=stride), :].astype(BF)
            full = dot(field, folded_ref[...], TN)
            re = full[:half, :unk] - full[half:, unk:]
            im = full[:half, unk:] + full[half:, :unk]
            out_ref[i] = jnp.concatenate([re, im], axis=1).astype(out_ref.dtype)


def receive_field(forward, folded, own, matrices, near, kinds):
    count = len(kinds)
    dirs, boxes, width = own.shape
    return pl.pallas_call(
        functools.partial(field_kernel, count, len(matrices)),
        out_shape=tuple(
            jax.ShapeDtypeStruct((boxes // count, width // 2, folded.shape[1]), kind)
            for kind in kinds
        ),
        in_specs=[VMEM] * (3 + len(matrices) + len(near)),
        out_specs=(VMEM,) * count,
        scratch_shapes=[
            pltpu.VMEM((dirs * (2 * boxes + 1), width), F32),
            pltpu.VMEM((dirs * (boxes + 1), width), F32),
        ],
        cost_estimate=cost(4 << 30, 16 << 20),
        name="field",
    )(forward, folded, own, *matrices, *near)


def mask_rows(values, live_counts):
    column = jnp.arange(values.shape[-1], dtype=I32) % (values.shape[-1] // 2)
    keep = column[None, None, :] < live_counts[:, None, None]
    return jnp.where(keep, values, jnp.zeros_like(values))


def body(
    currents,
    live_counts,
    radiation,
    sources,
    operator_ids,
    translators,
    stencil,
    stencil_weights,
    receiving,
):
    n_dir, n_grp = lax.axis_size("dir"), lax.axis_size("grp")
    dirs = translators.shape[2]
    per, incid, _ = currents.shape
    boxes = n_dir * per
    window = round_up(3 * boxes, LANES)
    place = jnp.stack([lax.axis_index("dir"), lax.axis_index("grp")]).astype(I32)

    def swap(values, bit):
        return lax.ppermute(values, "dir", [(i, i ^ bit) for i in range(n_dir)])

    def pair(values, odd):
        pairs = [(i, i + 1) for i in range(odd, n_grp - 1, 2)]
        return lax.ppermute(values, "grp", pairs + [(b, a) for a, b in pairs])

    shard, points = prepare(
        place, live_counts, stencil.T, stencil_weights.T, currents, radiation.shape[0]
    )
    slots = {0: shard}
    bit = n_dir // 2
    while bit:
        for j in sorted(slots):
            slots[j + bit] = swap(slots[j], bit)
        bit //= 2
    shards = [slots[j] for j in range(n_dir)]
    far = [pair(s, 1) for s in shards]
    near = [pair(s, 0) for s in shards]

    half = boxes // 2
    matrices = [
        transfer(place, sources, operator_ids, translators, first, half, per, window)
        for first in (0, half)
    ]
    own, forward, folded = own_pattern(place, radiation, receiving, points, shards, incid, dirs)
    kinds = [BF if j & 1 else F32 for j in range(n_dir)]
    parts = receive_field(forward, folded, own, matrices, far + near, kinds)
    sums = dict(enumerate(parts))
    bit = 1
    while bit < n_dir:
        for j in sorted((j for j in sums if j & bit), reverse=True):
            sums[j ^ bit] = sums[j ^ bit] + swap(sums.pop(j).astype(BF), bit).astype(F32)
        bit *= 2
    return mask_rows(sums[0], live_counts)


def solution(mesh):
    placed = (
        P(("grp", "dir"), None, None),
        P(("grp", "dir")),
        P(),
        P("grp", None),
        P("grp", None),
        P(None, None, "dir"),
        P("dir", None),
        P("dir", None),
        P(),
    )
    return jax.shard_map(
        body,
        mesh=mesh,
        in_specs=placed,
        out_specs=P(("grp", "dir"), None, None),
        check_vma=False,
    )
```

```python
import functools
import math

import jax
import jax.numpy as jnp
from jax import lax
from jax.experimental import pallas as pl
from jax.experimental.pallas import tpu as pltpu
from jax.sharding import PartitionSpec as P

RIM = 8
LANES = 128
BF = jnp.bfloat16
F32 = jnp.float32
I32 = jnp.int32
NT = (((1,), (1,)), ((), ()))
TN = (((0,), (0,)), ((), ()))
NN = (((1,), (0,)), ((), ()))
VMEM = pl.BlockSpec(memory_space=pltpu.VMEM)
SMEM = pl.BlockSpec(memory_space=pltpu.SMEM)


def round_up(value, unit):
    return -(-value // unit) * unit


def dot(a, b, dims):
    return lax.dot_general(a, b, dims, preferred_element_type=F32)


def cost(flops, nbytes):
    return pl.CostEstimate(flops=int(flops), bytes_accessed=int(nbytes), transcendentals=0)


def grant(*groups):
    size = 4 << 20
    for group in groups:
        for item in group:
            size += math.prod(item.shape) * jnp.dtype(item.dtype).itemsize
    return pltpu.CompilerParams(vmem_limit_bytes=min(size, 60 * 1024 * 1024))


def count_of(shape, axis):
    return lax.broadcasted_iota(I32, shape, axis)


def as_bf16(mask):
    return mask.astype(F32).astype(BF)


def unrolled(trips, most, step):
    size = next(n for n in range(min(most, trips), 0, -1) if trips % n == 0)

    def block(i, carry):
        for j in range(size):
            step(i * size + j)
        return carry

    lax.fori_loop(0, trips // size, block, 0)


def prepare_kernel(rim, all_dirs, place_ref, live_ref, stencil_ref, weight_ref, box_ref, out_ref, point_ref):
    boxes, incid, width = box_ref.shape
    points, dirs = stencil_ref.shape
    unk = count_of((incid, width), 1)
    unk = jnp.where(unk < width // 2, unk, unk - width // 2)
    for b in range(boxes):
        kept = jnp.where(unk < live_ref[b], box_ref[b].astype(F32), 0.0)
        out_ref[b * incid : (b + 1) * incid, :] = kept.astype(BF)
    away = stencil_ref[...] - (count_of((points, dirs), 1) + place_ref[0] * dirs)
    away = jnp.where(away > all_dirs // 2, away - all_dirs, away)
    away = jnp.where(away < -(all_dirs // 2), away + all_dirs, away)
    rows = jnp.concatenate([away.astype(F32), weight_ref[...].astype(F32)], axis=0)
    point_ref[...] = rows
    source, target = count_of((dirs, width), 0), count_of((dirs, width), 1)
    head = (target < rim) & (source == target)
    tail = (target >= rim) & (target < 2 * rim) & (source == target + dirs - 2 * rim)
    out_ref[boxes * incid :, :] = dot(rows.astype(BF), as_bf16(head | tail), NN).astype(BF)


def prepare(place, live_counts, stencil, weights, currents, all_dirs):
    boxes, incid, width = currents.shape
    points, dirs = stencil.shape
    return pl.pallas_call(
        functools.partial(prepare_kernel, RIM, all_dirs),
        out_shape=(
            jax.ShapeDtypeStruct((boxes * incid + 2 * points, width), BF),
            jax.ShapeDtypeStruct((2 * points, dirs), F32),
        ),
        in_specs=[SMEM, SMEM, VMEM, VMEM, VMEM],
        out_specs=(VMEM, VMEM),
        cost_estimate=cost(1 << 20, 1 << 20),
        name="prepare",
    )(place, live_counts, stencil, weights, currents)


def transfer_kernel(first, per, slots, place_ref, source_ref, kind_ref, table_ref, matrix_ref, lists, table, wide):
    all_boxes, width = source_ref.shape
    dirs, rows, window = matrix_ref.shape
    boxes = rows // 2
    kinds = table_ref.shape[0]
    padded = table.shape[1]
    own_dir, own_group = place_ref[0], place_ref[1]

    local = source_ref[...] - (own_group - 1) * all_boxes
    group = (local >= all_boxes).astype(I32) + (local >= 2 * all_boxes).astype(I32)
    inside = local - group * all_boxes
    holder = jnp.zeros_like(inside)
    for j in range(1, slots):
        holder += (inside >= j * per).astype(I32)
    paired = jnp.where(own_group % 2 == 0, 2, 0)
    turn = jnp.where(group == 1, 0, jnp.where(group == paired, 2, 1))
    spot = turn * all_boxes + (own_dir ^ holder) * per + inside - holder * per
    lists[...] = jnp.full(lists.shape, -1, I32)
    lists[:all_boxes, :width] = spot
    lists[all_boxes:, :width] = kind_ref[...]

    fill = jnp.zeros((padded - kinds, dirs), BF)
    for c in range(2):
        part = jnp.concatenate([table_ref[:, c, :], fill], axis=0)
        table[c * dirs : (c + 1) * dirs, :] = part.T

    lanes = lists.shape[1]

    def two_boxes(step):
        counts = []
        for i in range(2):
            at = first + 2 * step + i
            row = (own_dir ^ (at // per)) * per + at % per
            hit_kind = count_of((padded, lanes), 0) == lists[pl.ds(all_boxes + row, 1), :]
            hit_source = count_of((window, lanes), 0) == lists[pl.ds(row, 1), :]
            counts.append(dot(as_bf16(hit_kind), as_bf16(hit_source), NT))
        counts = jnp.concatenate(counts, axis=1).astype(BF)
        entries = dot(table[...], counts, NN)
        for i in range(2):
            for c in range(window // LANES):
                part = entries[:, i * window + c * LANES : i * window + (c + 1) * LANES]
                at = 2 * step + i
                wide[c, pl.ds(at, dirs, stride=rows + 1), :] = part[:dirs]
                wide[c, pl.ds(at + boxes, dirs, stride=rows + 1), :] = part[dirs:]

    unrolled(boxes // 2, 4, two_boxes)

    def narrow(k):
        for c in range(window // LANES):
            part = wide[c, pl.ds(k * (rows + 1), rows), :]
            matrix_ref[k, :, c * LANES : (c + 1) * LANES] = part.astype(BF)

    unrolled(dirs, 16, narrow)


def transfer(place, sources, operator_ids, translators, first, boxes, per, window):
    kinds, _, dirs = translators.shape
    all_boxes, width = sources.shape
    padded = round_up(kinds, LANES)
    out_shape = jax.ShapeDtypeStruct((dirs, 2 * boxes, window), BF)
    scratch = [
        pltpu.VMEM((2 * all_boxes, round_up(width, LANES)), I32),
        pltpu.VMEM((2 * dirs, padded), BF),
        pltpu.VMEM((window // LANES, dirs * (2 * boxes + 1), LANES), F32),
    ]
    return pl.pallas_call(
        functools.partial(transfer_kernel, first, per, all_boxes // per),
        out_shape=out_shape,
        in_specs=[SMEM, VMEM, VMEM, VMEM],
        out_specs=VMEM,
        scratch_shapes=scratch,
        compiler_params=grant(scratch, [out_shape, translators, translators]),
        cost_estimate=cost(8 << 30, 4 << 20),
        name="transfer",
    )(place, sources, operator_ids, translators)


def rotated(box):
    half = box.shape[1] // 2
    re, im = box[:, :half], box[:, half:]
    return jnp.concatenate(
        [jnp.concatenate([re, -im], axis=1), jnp.concatenate([im, re], axis=1)], axis=0
    )


def radiate(forward, box_refs, incid, out, stride):
    dirs = forward.shape[0]
    at = 0
    for ref in box_refs:
        for row in range(0, ref.shape[0] // incid * incid, 2 * incid):
            both = [rotated(ref[i : i + incid, :]) for i in (row, row + incid)]
            field = dot(forward[...], jnp.concatenate(both, axis=0), NT)
            out[pl.ds(at, dirs, stride=stride), :] = field[:, : 2 * incid]
            out[pl.ds(at + 1, dirs, stride=stride), :] = field[:, 2 * incid :]
            at += 2


def pattern_kernel(
    count, incid, rim, place_ref, forward_ref, receive_ref, after_ref, before_ref, point_ref, *refs
):
    box_refs, (pattern_ref, turned_ref, folded_ref, wide) = refs[:count], refs[count:]
    dirs, boxes, _ = pattern_ref.shape
    turned_ref[...] = jnp.concatenate([forward_ref[:, 0, :], forward_ref[:, 1, :]], axis=1)
    radiate(turned_ref, box_refs, incid, wide, boxes + 1)

    def narrow(k):
        pattern_ref[k] = wide[pl.ds(k * (boxes + 1), boxes), :].astype(BF)

    unrolled(dirs, 16, narrow)

    own_dir = place_ref[0]
    points = point_ref.shape[0] // 2
    lane = count_of((2 * points, LANES), 1)
    ends = jnp.zeros((2 * points, LANES), F32)
    for j, ref in enumerate(box_refs):
        tail = ref[ref.shape[0] - 2 * points :, :LANES].astype(F32)
        holder = own_dir ^ j
        follows = holder == lax.rem(own_dir + 1, count)
        leads = holder == lax.rem(own_dir + count - 1, count)
        here = ((lane < rim) & follows) | ((lane >= rim) & (lane < 2 * rim) & leads)
        ends = jnp.where(here, tail, ends)
    spot = count_of((points, LANES), 1)
    spot = jnp.where(spot < rim, spot + dirs, spot - 2 * rim)
    spots = [point_ref[:points, :].astype(I32) + count_of((points, dirs), 1)]
    spots.append(ends[:points].astype(I32) + spot)
    gains = [point_ref[points:, :], ends[points:]]
    tables = [receive_ref[...], jnp.concatenate([after_ref[...], before_ref[...]], axis=0)]
    folded = None
    for spot, gain, table in zip(spots, gains, tables):
        extent = spot.shape[1]
        own = count_of((dirs, extent), 0)
        spread = jnp.zeros((dirs, extent), F32)
        for p in range(points):
            spread += jnp.where(own == spot[p : p + 1, :], gain[p : p + 1, :], 0.0)
        flat = jnp.concatenate([table[:, 0, :], table[:, 1, :]], axis=1)
        if flat.shape[0] < extent:
            blank = jnp.zeros((extent - flat.shape[0], flat.shape[1]), BF)
            flat = jnp.concatenate([flat, blank], axis=0)
        part = dot(spread.astype(BF), flat, NN)
        folded = part if folded is None else folded + part
    folded_ref[...] = folded.astype(BF)


def own_pattern(place, radiation, receiving, rows, shards, incid, dirs):
    count = len(shards)
    boxes = sum(s.shape[0] // incid for s in shards)
    all_dirs, parts, unk = receiving.shape
    own = pl.BlockSpec((dirs, parts, unk), lambda i, at: (at[0], 0, 0))
    rims, total = dirs // RIM, all_dirs // RIM
    after = pl.BlockSpec((RIM, parts, unk), lambda i, at: (lax.rem((at[0] + 1) * rims, total), 0, 0))
    before = pl.BlockSpec(
        (RIM, parts, unk), lambda i, at: (lax.rem(at[0] * rims + total - 1, total), 0, 0)
    )
    out_shape = (
        jax.ShapeDtypeStruct((dirs, boxes, 2 * incid), BF),
        jax.ShapeDtypeStruct((dirs, parts * unk), BF),
        jax.ShapeDtypeStruct((dirs, parts * unk), BF),
    )
    scratch = [pltpu.VMEM((dirs * (boxes + 1), 2 * incid), F32)]
    return pl.pallas_call(
        functools.partial(pattern_kernel, count, incid, RIM),
        out_shape=out_shape,
        grid_spec=pltpu.PrefetchScalarGridSpec(
            num_scalar_prefetch=1,
            grid=(1,),
            in_specs=[own, own, after, before] + [VMEM] * (1 + count),
            out_specs=(VMEM, VMEM, VMEM),
            scratch_shapes=scratch,
        ),
        compiler_params=grant(scratch, out_shape, out_shape, shards, shards),
        cost_estimate=cost(1 << 30, 4 << 20),
        name="pattern",
    )(place, radiation, receiving, receiving, receiving, rows, *shards)


def field_kernel(count, halves, forward_ref, folded_ref, own_ref, *refs):
    matrix_refs, refs = refs[:halves], refs[halves:]
    box_refs, out_refs, (near, moved) = refs[: -count - 2], refs[-count - 2 : -2], refs[-2:]
    dirs, own_boxes, width = own_ref.shape
    near_boxes = 2 * own_boxes
    boxes = matrix_refs[0].shape[1] // 2
    half = width // 2
    radiate(forward_ref, box_refs, half, near, near_boxes + 1)
    sign = jnp.where(count_of((boxes, width), 1) < half, -1.0, 1.0).astype(F32)
    stride = own_boxes + 1

    def translate(k):
        around = near[pl.ds(k * (near_boxes + 1), near_boxes), :].astype(BF)
        fields = jnp.concatenate([own_ref[k], around], axis=0)
        weights = [ref[k][:, : own_boxes + near_boxes] for ref in matrix_refs]
        both = dot(jnp.concatenate(weights, axis=0), fields, NN)
        for h in range(halves):
            part = both[2 * boxes * h : 2 * boxes * (h + 1)]
            turned = pltpu.roll(part[boxes:], half, 1)
            moved[pl.ds(k * stride + h * boxes, boxes), :] = part[:boxes] + sign * turned

    unrolled(dirs, 64 * 32 // own_boxes, translate)

    unk = folded_ref.shape[1] // 2
    per = own_boxes // count
    for j, out_ref in enumerate(out_refs):
        for i in range(per):
            field = moved[pl.ds(j * per + i, dirs, stride=stride), :].astype(BF)
            full = dot(field, folded_ref[...], TN)
            re = full[:half, :unk] - full[half:, unk:]
            im = full[:half, unk:] + full[half:, :unk]
            out_ref[i] = jnp.concatenate([re, im], axis=1).astype(out_ref.dtype)


def receive_field(forward, folded, own, matrices, near, kinds):
    count = len(kinds)
    dirs, boxes, width = own.shape
    out_shape = tuple(
        jax.ShapeDtypeStruct((boxes // count, width // 2, folded.shape[1]), kind) for kind in kinds
    )
    scratch = [
        pltpu.VMEM((dirs * (2 * boxes + 1), width), F32),
        pltpu.VMEM((dirs * (boxes + 1), width), F32),
    ]
    return pl.pallas_call(
        functools.partial(field_kernel, count, len(matrices)),
        out_shape=out_shape,
        in_specs=[VMEM] * (3 + len(matrices) + len(near)),
        out_specs=(VMEM,) * count,
        scratch_shapes=scratch,
        compiler_params=grant(scratch, out_shape, [forward, folded, own], matrices, near),
        cost_estimate=cost(4 << 30, 16 << 20),
        name="field",
    )(forward, folded, own, *matrices, *near)


def mask_rows(values, live_counts):
    column = jnp.arange(values.shape[-1], dtype=I32) % (values.shape[-1] // 2)
    keep = column[None, None, :] < live_counts[:, None, None]
    return jnp.where(keep, values, jnp.zeros_like(values))


def body(
    currents,
    live_counts,
    radiation,
    sources,
    operator_ids,
    translators,
    stencil,
    stencil_weights,
    receiving,
):
    n_dir, n_grp = lax.axis_size("dir"), lax.axis_size("grp")
    dirs = translators.shape[2]
    per, incid, _ = currents.shape
    boxes = n_dir * per
    window = round_up(3 * boxes, LANES)
    place = jnp.stack([lax.axis_index("dir"), lax.axis_index("grp")]).astype(I32)

    def swap(values, bit):
        return lax.ppermute(values, "dir", [(i, i ^ bit) for i in range(n_dir)])

    def pair(values, odd):
        pairs = [(i, i + 1) for i in range(odd, n_grp - 1, 2)]
        return lax.ppermute(values, "grp", pairs + [(b, a) for a, b in pairs])

    shard, points = prepare(
        place, live_counts, stencil.T, stencil_weights.T, currents, radiation.shape[0]
    )
    slots = {0: shard}
    bit = n_dir // 2
    while bit:
        for j in sorted(slots):
            slots[j + bit] = swap(slots[j], bit)
        bit //= 2
    shards = [slots[j] for j in range(n_dir)]
    far = [pair(s, 1) for s in shards]
    near = [pair(s, 0) for s in shards]

    half = boxes // 2
    matrices = [
        transfer(place, sources, operator_ids, translators, first, half, per, window)
        for first in (0, half)
    ]
    own, forward, folded = own_pattern(place, radiation, receiving, points, shards, incid, dirs)
    kinds = [BF if j & 1 else F32 for j in range(n_dir)]
    parts = receive_field(forward, folded, own, matrices, far + near, kinds)
    sums = dict(enumerate(parts))
    bit = 1
    while bit < n_dir:
        for j in sorted((j for j in sums if j & bit), reverse=True):
            sums[j ^ bit] = sums[j ^ bit] + swap(sums.pop(j).astype(BF), bit).astype(F32)
        bit *= 2
    return mask_rows(sums[0], live_counts)


def solution(mesh):
    placed = (
        P(("grp", "dir"), None, None),
        P(("grp", "dir")),
        P(),
        P("grp", None),
        P("grp", None),
        P(None, None, "dir"),
        P("dir", None),
        P("dir", None),
        P(),
    )
    return jax.shard_map(
        body,
        mesh=mesh,
        in_specs=placed,
        out_specs=P(("grp", "dir"), None, None),
        check_vma=False,
    )
```

```python
import functools
import math

import jax
import jax.numpy as jnp
from jax import lax
from jax.experimental import pallas as pl
from jax.experimental.pallas import tpu as pltpu
from jax.sharding import PartitionSpec as P

RIM = 8
LANES = 128
BF = jnp.bfloat16
F32 = jnp.float32
I32 = jnp.int32
NT = (((1,), (1,)), ((), ()))
TN = (((0,), (0,)), ((), ()))
NN = (((1,), (0,)), ((), ()))
VMEM = pl.BlockSpec(memory_space=pltpu.VMEM)
SMEM = pl.BlockSpec(memory_space=pltpu.SMEM)


def round_up(value, unit):
    return -(-value // unit) * unit


def dot(a, b, dims):
    return lax.dot_general(a, b, dims, preferred_element_type=F32)


def cost(flops, nbytes):
    return pl.CostEstimate(flops=int(flops), bytes_accessed=int(nbytes), transcendentals=0)


def grant(*groups):
    size = 4 << 20
    for group in groups:
        for item in group:
            size += math.prod(item.shape) * jnp.dtype(item.dtype).itemsize
    return pltpu.CompilerParams(vmem_limit_bytes=min(size, 60 * 1024 * 1024))


def count_of(shape, axis):
    return lax.broadcasted_iota(I32, shape, axis)


def as_bf16(mask):
    return mask.astype(F32).astype(BF)


def unrolled(trips, most, step):
    size = next(n for n in range(min(most, trips), 0, -1) if trips % n == 0)

    def block(i, carry):
        for j in range(size):
            step(i * size + j)
        return carry

    lax.fori_loop(0, trips // size, block, 0)


def prepare_kernel(all_dirs, place_ref, live_ref, stencil_ref, weight_ref, box_ref, out_ref):
    boxes, incid, width = box_ref.shape
    points, dirs = stencil_ref.shape
    unk = count_of((incid, width), 1)
    unk = jnp.where(unk < width // 2, unk, unk - width // 2)
    for b in range(boxes):
        kept = jnp.where(unk < live_ref[b], box_ref[b].astype(F32), 0.0)
        out_ref[b * incid : (b + 1) * incid, :] = kept.astype(BF)
    away = stencil_ref[...] - (count_of((points, dirs), 1) + place_ref[0] * dirs)
    away = jnp.where(away > all_dirs // 2, away - all_dirs, away)
    away = jnp.where(away < -(all_dirs // 2), away + all_dirs, away)
    rows = jnp.concatenate([away.astype(F32), weight_ref[...].astype(F32)], axis=0)
    if dirs < width:
        rows = jnp.concatenate([rows, jnp.zeros((2 * points, width - dirs), F32)], axis=1)
    out_ref[boxes * incid :, :] = rows.astype(BF)


def prepare(place, live_counts, stencil, weights, currents, all_dirs):
    boxes, incid, width = currents.shape
    points, dirs = stencil.shape
    out_shape = jax.ShapeDtypeStruct((boxes * incid + 2 * points, width), BF)
    return pl.pallas_call(
        functools.partial(prepare_kernel, all_dirs),
        out_shape=out_shape,
        in_specs=[SMEM, SMEM, VMEM, VMEM, VMEM],
        out_specs=VMEM,
        compiler_params=grant([out_shape, currents]),
        cost_estimate=cost(1 << 20, 1 << 20),
        name="prepare",
    )(place, live_counts, stencil, weights, currents)


def counts_kernel(slots, place_ref, source_ref, kind_ref, counts_ref, lists):
    all_boxes, width = source_ref.shape
    per = all_boxes // slots
    padded, lanes_out = counts_ref.shape
    window = lanes_out // (2 * per)
    own_dir, own_group = place_ref[0], place_ref[1]
    lists[...] = jnp.full(lists.shape, -1, I32)
    for i in range(2):
        first = pl.multiple_of((own_dir ^ i) * per, 8)
        local = source_ref[pl.ds(first, per), :] - (own_group - 1) * all_boxes
        group = (local >= all_boxes).astype(I32) + (local >= 2 * all_boxes).astype(I32)
        inside = local - group * all_boxes
        holder = jnp.zeros_like(inside)
        for j in range(1, slots):
            holder += (inside >= j * per).astype(I32)
        slot = own_dir ^ holder
        side = jnp.where(group == 0, 0, 1)
        around = jnp.where(slot < 2, 2 * slots - 2 + 2 * slot + side, slots - 2 + slot)
        slot = jnp.where(group == 1, slot, around)
        lists[i * per : (i + 1) * per, :width] = slot * per + inside - holder * per
        lists[(2 + i) * per : (3 + i) * per, :width] = kind_ref[pl.ds(first, per), :]
    lanes = lists.shape[1]
    for i in range(2 * per):
        hit_kind = count_of((padded, lanes), 0) == lists[2 * per + i : 2 * per + i + 1, :]
        hit_source = count_of((window, lanes), 0) == lists[i : i + 1, :]
        counts = dot(as_bf16(hit_kind), as_bf16(hit_source), NT)
        counts_ref[:, i * window : (i + 1) * window] = counts.astype(BF)


def count_entries(place, sources, operator_ids, kinds, slots, window):
    all_boxes, width = sources.shape
    boxes = 2 * (all_boxes // slots)
    out_shape = jax.ShapeDtypeStruct((round_up(kinds, LANES), boxes * window), BF)
    scratch = [pltpu.VMEM((2 * boxes, round_up(width, LANES)), I32)]
    return pl.pallas_call(
        functools.partial(counts_kernel, slots),
        out_shape=out_shape,
        in_specs=[SMEM, VMEM, VMEM],
        out_specs=VMEM,
        scratch_shapes=scratch,
        compiler_params=grant(scratch, [out_shape, sources, sources]),
        cost_estimate=cost(1 << 30, 1 << 20),
        name="counts",
    )(place, sources, operator_ids)


def transfer_kernel(counts_ref, table_ref, matrix_ref, table, wide):
    dirs, rows, window = matrix_ref.shape
    boxes = rows // 2
    kinds = table_ref.shape[0]
    fill = jnp.zeros((table.shape[1] - kinds, dirs), BF)
    for c in range(2):
        part = jnp.concatenate([table_ref[:, c, :], fill], axis=0)
        table[c * dirs : (c + 1) * dirs, :] = part.T
    for at in range(0, boxes, 2):
        entries = dot(table[...], counts_ref[:, at * window : (at + 2) * window], NN)
        for i in range(2):
            for c in range(window // LANES):
                part = entries[:, i * window + c * LANES : i * window + (c + 1) * LANES]
                wide[c, pl.ds(at + i, dirs, stride=rows + 1), :] = part[:dirs]
                wide[c, pl.ds(at + i + boxes, dirs, stride=rows + 1), :] = part[dirs:]

    def narrow(k):
        for c in range(window // LANES):
            part = wide[c, pl.ds(k * (rows + 1), rows), :]
            matrix_ref[k, :, c * LANES : (c + 1) * LANES] = part.astype(BF)

    unrolled(dirs, 64, narrow)


def transfer(counts, translators, per, window):
    kinds, _, dirs = translators.shape
    out_shape = jax.ShapeDtypeStruct((dirs, 2 * per, window), BF)
    scratch = [
        pltpu.VMEM((2 * dirs, counts.shape[0]), BF),
        pltpu.VMEM((window // LANES, dirs * (2 * per + 1), LANES), F32),
    ]
    return pl.pallas_call(
        transfer_kernel,
        out_shape=out_shape,
        in_specs=[VMEM, VMEM],
        out_specs=VMEM,
        scratch_shapes=scratch,
        compiler_params=grant(scratch, [out_shape, translators, translators, counts]),
        cost_estimate=cost(1 << 30, 1 << 20),
        name="transfer",
    )(counts, translators)


def rotated(box):
    half = box.shape[1] // 2
    re, im = box[:, :half], box[:, half:]
    return jnp.concatenate(
        [jnp.concatenate([re, -im], axis=1), jnp.concatenate([im, re], axis=1)], axis=0
    )


def radiate(forward, box_refs, incid, out, stride):
    dirs = forward.shape[0]
    at = 0
    for ref in box_refs:
        for row in range(0, ref.shape[0] // incid * incid, 2 * incid):
            both = [rotated(ref[i : i + incid, :]) for i in (row, row + incid)]
            field = dot(forward[...], jnp.concatenate(both, axis=0), NT)
            out[pl.ds(at, dirs, stride=stride), :] = field[:, : 2 * incid]
            out[pl.ds(at + 1, dirs, stride=stride), :] = field[:, 2 * incid :]
            at += 2


def pattern_kernel(slots, count, incid, rim, place_ref, *refs):
    forward_refs, refs = refs[: len(slots)], refs[len(slots) :]
    receive_ref, refs = refs[0], refs[1:]
    box_refs, (pattern_ref, turned_ref, folded_ref, wide, tails) = refs[:count], refs[count:]
    rows, boxes, _ = pattern_ref.shape
    dirs = rows // len(slots)
    for j, ref in enumerate(forward_refs):
        flat = jnp.concatenate([ref[:, 0, :], ref[:, 1, :]], axis=1)
        turned_ref[j * dirs : (j + 1) * dirs, :] = flat
    radiate(turned_ref, box_refs, incid, wide, boxes + 1)

    def narrow(k):
        pattern_ref[k] = wide[pl.ds(k * (boxes + 1), boxes), :].astype(BF)

    unrolled(rows, 32, narrow)

    own_dir = place_ref[0]
    points = tails.shape[1] // 2
    total = receive_ref.shape[0]
    for j, ref in enumerate(box_refs):
        tails[j] = ref[ref.shape[0] - 2 * points :, :].astype(F32)
    lane = count_of((2 * points, LANES), 1)
    source = count_of((tails.shape[2], LANES), 0)
    target = count_of((tails.shape[2], LANES), 1)
    head = as_bf16((target < rim) & (source == target))
    tail = as_bf16((target >= rim) & (target < 2 * rim) & (source == target + dirs - 2 * rim))
    for at, j in enumerate(slots):
        holder = own_dir ^ j
        follows = own_dir ^ lax.rem(holder + 1, count)
        leads = own_dir ^ lax.rem(holder + count - 1, count)
        ends = dot(tails[follows].astype(BF), head, NN) + dot(tails[leads].astype(BF), tail, NN)
        here = tails[j][:, :dirs]
        spot = count_of((points, LANES), 1)
        spot = jnp.where(spot < rim, spot + dirs, spot - 2 * rim)
        spots = [here[:points].astype(I32) + count_of((points, dirs), 1)]
        spots.append(ends[:points].astype(I32) + spot)
        gains = [here[points:], ends[points:]]
        start = holder * dirs
        after = receive_ref[pl.ds(lax.rem(start + dirs, total), rim)]
        before = receive_ref[pl.ds(lax.rem(start + total - rim, total), rim)]
        tables = [receive_ref[pl.ds(start, dirs)], jnp.concatenate([after, before], axis=0)]
        folded = None
        for spot, gain, table in zip(spots, gains, tables):
            extent = spot.shape[1]
            own = count_of((dirs, extent), 0)
            spread = jnp.zeros((dirs, extent), F32)
            for p in range(points):
                spread += jnp.where(own == spot[p : p + 1, :], gain[p : p + 1, :], 0.0)
            flat = jnp.concatenate([table[:, 0, :], table[:, 1, :]], axis=1)
            if flat.shape[0] < extent:
                blank = jnp.zeros((extent - flat.shape[0], flat.shape[1]), BF)
                flat = jnp.concatenate([flat, blank], axis=0)
            part = dot(spread.astype(BF), flat, NN)
            folded = part if folded is None else folded + part
        folded_ref[at * dirs : (at + 1) * dirs, :] = folded.astype(BF)


def own_pattern(place, radiation, receiving, shards, slots, incid, points, dirs):
    count = len(shards)
    boxes = sum(s.shape[0] // incid for s in shards)
    all_dirs, parts, unk = receiving.shape
    rows = len(slots) * dirs
    blocks = [
        pl.BlockSpec((dirs, parts, unk), lambda i, at, j=j: (at[0] ^ j, 0, 0)) for j in slots
    ]
    out_shape = (
        jax.ShapeDtypeStruct((rows, boxes, 2 * incid), BF),
        jax.ShapeDtypeStruct((rows, parts * unk), BF),
        jax.ShapeDtypeStruct((rows, parts * unk), BF),
    )
    scratch = [
        pltpu.VMEM((rows * (boxes + 1), 2 * incid), F32),
        pltpu.VMEM((count, 2 * points, shards[0].shape[1]), F32),
    ]
    return pl.pallas_call(
        functools.partial(pattern_kernel, slots, count, incid, RIM),
        out_shape=out_shape,
        grid_spec=pltpu.PrefetchScalarGridSpec(
            num_scalar_prefetch=1,
            grid=(1,),
            in_specs=blocks + [VMEM] * (1 + count),
            out_specs=(VMEM, VMEM, VMEM),
            scratch_shapes=scratch,
        ),
        compiler_params=grant(scratch, out_shape, shards, [radiation, radiation, receiving]),
        cost_estimate=cost(4 << 30, 4 << 20),
        name="pattern",
    )(place, *[radiation] * len(slots), receiving, *shards)


def field_kernel(slices, live_ref, forward_ref, folded_ref, own_ref, *refs):
    matrix_refs, refs = refs[:slices], refs[slices:]
    box_refs, (out_ref, pair_ref, near, moved) = refs[:-4], refs[-4:]
    rows, own_boxes, width = own_ref.shape
    per, half, _ = out_ref.shape
    boxes = 2 * per
    near_boxes = len(box_refs) * per
    radiate(forward_ref, box_refs, half, near, near_boxes + 1)
    sign = jnp.where(count_of((boxes, width), 1) < half, -1.0, 1.0).astype(F32)
    stride = boxes + 1
    dirs = rows // slices
    for at, matrix_ref in enumerate(matrix_refs):

        def translate(i, at=at, matrix_ref=matrix_ref):
            k = at * dirs + i
            around = near[pl.ds(k * (near_boxes + 1), near_boxes), :].astype(BF)
            fields = jnp.concatenate([own_ref[k], around], axis=0)
            both = dot(matrix_ref[i][:, : own_boxes + near_boxes], fields, NN)
            turned = pltpu.roll(both[boxes:], half, 1)
            moved[pl.ds(k * stride, boxes), :] = both[:boxes] + sign * turned

        unrolled(dirs, 64, translate)

    unk = folded_ref.shape[1] // 2
    lane = count_of((half, unk), 1)
    for i in reversed(range(boxes)):
        field = moved[pl.ds(i, rows, stride=stride), :].astype(BF)
        full = dot(field, folded_ref[...], TN)
        re = full[:half, :unk] - full[half:, unk:]
        im = full[:half, unk:] + full[half:, :unk]
        both = jnp.concatenate([re, im], axis=1)
        if i < per:
            out_ref[i] = both
        else:
            pair_ref[i - per] = both.astype(pair_ref.dtype)


def receive_field(live_counts, forward, folded, own, matrices, near, kind):
    rows, _, width = own.shape
    per = matrices[0].shape[1] // 4
    shape = (per, width // 2, folded.shape[1])
    out_shape = (jax.ShapeDtypeStruct(shape, F32), jax.ShapeDtypeStruct(shape, kind))
    scratch = [
        pltpu.VMEM((rows * (len(near) * per + 1), width), F32),
        pltpu.VMEM((rows * (2 * per + 1), width), F32),
    ]
    return pl.pallas_call(
        functools.partial(field_kernel, len(matrices)),
        out_shape=out_shape,
        in_specs=[SMEM] + [VMEM] * (3 + len(matrices) + len(near)),
        out_specs=(VMEM, VMEM),
        scratch_shapes=scratch,
        compiler_params=grant(scratch, out_shape, [forward, folded, own], matrices, near),
        cost_estimate=cost(4 << 30, 16 << 20),
        name="field",
    )(live_counts, forward, folded, own, *matrices, *near)


def mask_rows(values, live_counts):
    column = jnp.arange(values.shape[-1], dtype=I32) % (values.shape[-1] // 2)
    keep = column[None, None, :] < live_counts[:, None, None]
    return jnp.where(keep, values, jnp.zeros_like(values))


def body(
    currents,
    live_counts,
    radiation,
    sources,
    operator_ids,
    translators,
    stencil,
    stencil_weights,
    receiving,
):
    n_dir, n_grp = lax.axis_size("dir"), lax.axis_size("grp")
    kinds, _, dirs = translators.shape
    per, incid, _ = currents.shape
    points = stencil.shape[1]
    window = round_up((2 * n_dir + 2) * per, LANES)
    place = jnp.stack([lax.axis_index("dir"), lax.axis_index("grp")]).astype(I32)

    def swap(values, bit):
        return lax.ppermute(values, "dir", [(i, i ^ bit) for i in range(n_dir)])

    def gather(values, last):
        slots = {0: values}
        bit = n_dir // 2
        while bit >= last:
            for j in sorted(slots):
                slots[j + bit] = swap(slots[j], bit)
            bit //= 2
        return [slots[j] for j in sorted(slots)]

    def across(values, step_of):
        pairs = []
        for g in range(n_grp):
            for d in range(n_dir):
                to = g + step_of(d)
                if 0 <= to < n_grp:
                    pairs.append((g * n_dir + d, to * n_dir + d))
        return lax.ppermute(values, ("grp", "dir"), pairs)

    shard = prepare(
        place, live_counts, stencil.T, stencil_weights.T, currents, radiation.shape[0]
    )
    shards = gather(shard, 1)
    near = [across(shards[j], lambda d, j=j: 1 if d ^ j > d else -1) for j in range(2, n_dir)]
    near += [across(shards[j], lambda d, step=step: step) for j in range(2) for step in (1, -1)]
    tables = gather(translators, 2)

    counts = count_entries(place, sources, operator_ids, kinds, n_dir, window)
    matrices = [transfer(counts, table, 2 * per, window) for table in tables]
    wide = dirs * (len(near) * per + 1) * LANES * 4
    slices = len(tables)
    size = max(n for n in range(1, slices + 1) if slices % n == 0 and (n == 1 or n * wide <= 24 << 20))
    sums = None
    for first in range(0, slices, size):
        own, forward, folded = own_pattern(
            place,
            radiation,
            receiving,
            shards,
            [2 * j for j in range(first, first + size)],
            incid,
            points,
            dirs,
        )
        part = receive_field(
            live_counts,
            forward,
            folded,
            own,
            matrices[first : first + size],
            near,
            BF if size == slices else F32,
        )
        sums = part if sums is None else [a + b for a, b in zip(sums, part)]
    total = sums[0] + swap(sums[1].astype(BF), 1).astype(F32)
    return mask_rows(total, live_counts)


def solution(mesh):
    placed = (
        P(("grp", "dir"), None, None),
        P(("grp", "dir")),
        P(),
        P("grp", None),
        P("grp", None),
        P(None, None, "dir"),
        P("dir", None),
        P("dir", None),
        P(),
    )
    return jax.shard_map(
        body,
        mesh=mesh,
        in_specs=placed,
        out_specs=P(("grp", "dir"), None, None),
        check_vma=False,
    )
```

```python
import functools
import math

import jax
import jax.numpy as jnp
from jax import lax
from jax.experimental import pallas as pl
from jax.experimental.pallas import tpu as pltpu
from jax.sharding import PartitionSpec as P


RIM = 8
LANES = 128
BF = jnp.bfloat16
F32 = jnp.float32
I32 = jnp.int32
NT = (((1,), (1,)), ((), ()))
TN = (((0,), (0,)), ((), ()))
NN = (((1,), (0,)), ((), ()))
VMEM = pl.BlockSpec(memory_space=pltpu.VMEM)
SMEM = pl.BlockSpec(memory_space=pltpu.SMEM)


def round_up(value, unit):
    return -(-value // unit) * unit


def half_of(kinds):
    return (kinds + 1) // 2


def table_rows(kinds):
    return round_up(2 * round_up(half_of(kinds), 16), LANES)


def dot(a, b, dims):
    return lax.dot_general(a, b, dims, preferred_element_type=F32)


def cost(flops, nbytes):
    return pl.CostEstimate(flops=int(flops), bytes_accessed=int(nbytes), transcendentals=0)


def grant(*groups):
    size = 4 << 20
    for group in groups:
        for item in group:
            size += math.prod(item.shape) * jnp.dtype(item.dtype).itemsize
    return pltpu.CompilerParams(vmem_limit_bytes=min(size, 60 * 1024 * 1024))


def count_of(shape, axis):
    return lax.broadcasted_iota(I32, shape, axis)


def as_bf16(mask):
    return mask.astype(F32).astype(BF)


def unrolled(trips, most, step):
    size = next(n for n in range(min(most, trips), 0, -1) if trips % n == 0)

    def block(i, carry):
        for j in range(size):
            step(i * size + j)
        return carry

    lax.fori_loop(0, trips // size, block, 0)


def prepare_kernel(all_dirs, live_ref, stencil_ref, weight_ref, box_ref, table_ref, out_ref, half_ref, sem):
    boxes, incid, width = box_ref.shape
    points, dirs = stencil_ref.shape
    half = half_ref.shape[0]
    first = lax.rem(lax.axis_index("grp"), 2) * (table_ref.shape[0] - half)
    fetch = pltpu.make_async_copy(table_ref.at[pl.ds(first, half)], half_ref, sem)
    fetch.start()
    unk = count_of((incid, width), 1)
    unk = jnp.where(unk < width // 2, unk, unk - width // 2)
    for b in range(boxes):
        kept = jnp.where(unk < live_ref[b], box_ref[b].astype(F32), 0.0)
        out_ref[b * incid : (b + 1) * incid, :] = kept.astype(BF)
    away = stencil_ref[...] - (count_of((points, dirs), 1) + lax.axis_index("dir") * dirs)
    away = jnp.where(away > all_dirs // 2, away - all_dirs, away)
    away = jnp.where(away < -(all_dirs // 2), away + all_dirs, away)
    rows = jnp.concatenate([away.astype(F32), weight_ref[...].astype(F32)], axis=0)
    if dirs < width:
        rows = jnp.concatenate([rows, jnp.zeros((2 * points, width - dirs), F32)], axis=1)
    out_ref[boxes * incid :, :] = rows.astype(BF)
    fetch.wait()


def prepare(live_counts, stencil, weights, currents, translators, all_dirs):
    boxes, incid, width = currents.shape
    points, dirs = stencil.shape
    kinds, parts, _ = translators.shape
    return pl.pallas_call(
        functools.partial(prepare_kernel, all_dirs),
        out_shape=(
            jax.ShapeDtypeStruct((boxes * incid + 2 * points, width), BF),
            jax.ShapeDtypeStruct((half_of(kinds), parts, dirs), BF),
        ),
        in_specs=[SMEM, VMEM, VMEM, VMEM, pl.BlockSpec(memory_space=pl.ANY)],
        out_specs=(VMEM, VMEM),
        scratch_shapes=[pltpu.SemaphoreType.DMA],
        cost_estimate=cost(1 << 20, 1 << 20),
        name="prepare",
    )(live_counts, stencil, weights, currents, translators)


def count_entries(slots, kinds, window, place_ref, source_ref, kind_ref, counts_ref, lists):
    all_boxes, width = source_ref.shape
    per = all_boxes // slots
    own_dir, own_group = place_ref[0], place_ref[1]
    half = half_of(kinds)
    lists[...] = jnp.full(lists.shape, -1, I32)
    for i in range(2):
        first = pl.multiple_of((own_dir ^ i) * per, 8)
        local = source_ref[pl.ds(first, per), :] - (own_group - 1) * all_boxes
        group = (local >= all_boxes).astype(I32) + (local >= 2 * all_boxes).astype(I32)
        inside = local - group * all_boxes
        holder = jnp.zeros_like(inside)
        for j in range(1, slots):
            holder += (inside >= j * per).astype(I32)
        slot = own_dir ^ holder
        side = jnp.where(group == jnp.where(own_group % 2 == 0, 2, 0), 1, 0)
        around = jnp.where(slot < 2, slots + 2 * slot + side, slots + 2 + slot)
        slot = jnp.where(group == 1, slot, around)
        lists[i * per : (i + 1) * per, :width] = slot * per + inside - holder * per
        kind = kind_ref[pl.ds(first, per), :]
        upper = kind - (kinds - half) + round_up(half, 16)
        kind = jnp.where(kind < half, kind, upper)
        lists[(2 + i) * per : (3 + i) * per, :width] = kind
    lanes = lists.shape[1]
    used = 2 * round_up(half, 16)
    if used < counts_ref.shape[0]:
        rest = (counts_ref.shape[0] - used, counts_ref.shape[1])
        counts_ref[used:, :] = jnp.zeros(rest, BF)
    for i in range(2 * per):
        hit_kind = count_of((used, lanes), 0) == lists[2 * per + i : 2 * per + i + 1, :]
        hit_source = count_of((window, lanes), 0) == lists[i : i + 1, :]
        counts = dot(as_bf16(hit_kind), as_bf16(hit_source), NT)
        counts_ref[:used, i * window : (i + 1) * window] = counts.astype(BF)


def fill_matrix(low, high, counts_ref, matrix_ref, table, wide):
    dirs, rows, window = matrix_ref.shape
    boxes = rows // 2
    half = low.shape[0]
    gap = round_up(half, 16) - half
    for c in range(2):
        fill = jnp.zeros((table.shape[1] - 2 * half - gap, dirs), BF)
        blank = jnp.zeros((gap, dirs), BF)
        part = jnp.concatenate([low[:, c, :], blank, high[:, c, :], fill], axis=0)
        table[c * dirs : (c + 1) * dirs, :] = part.T
    for at in range(0, boxes, 2):
        entries = dot(table[...], counts_ref[:, at * window : (at + 2) * window], NN)
        for i in range(2):
            for c in range(window // LANES):
                part = entries[:, i * window + c * LANES : i * window + (c + 1) * LANES]
                wide[c, pl.ds(at + i, dirs, stride=rows + 1), :] = part[:dirs]
                wide[c, pl.ds(at + i + boxes, dirs, stride=rows + 1), :] = part[dirs:]

    def narrow(k):
        for c in range(window // LANES):
            part = wide[c, pl.ds(k * (rows + 1), rows), :]
            matrix_ref[k, :, c * LANES : (c + 1) * LANES] = part.astype(BF)

    unrolled(dirs, 64, narrow)


def first_kernel(slots, place_ref, source_hbm, kind_hbm, table_hbm, counts_ref, matrix_ref, *scratch):
    source_ref, kind_ref, table_ref, lists, table, wide, sems = scratch
    window = matrix_ref.shape[2]
    kinds = table_ref.shape[0]
    copies = [
        pltpu.make_async_copy(source_hbm, source_ref, sems.at[0]),
        pltpu.make_async_copy(kind_hbm, kind_ref, sems.at[1]),
        pltpu.make_async_copy(table_hbm, table_ref, sems.at[2]),
    ]
    for copy in copies:
        copy.start()
    copies[0].wait()
    copies[1].wait()
    count_entries(slots, kinds, window, place_ref, source_ref, kind_ref, counts_ref, lists)
    copies[2].wait()
    half = half_of(kinds)
    low, high = table_ref.at[pl.ds(0, half)], table_ref.at[pl.ds(kinds - half, half)]
    fill_matrix(low, high, counts_ref, matrix_ref, table, wide)


def first_transfer(place, sources, operator_ids, translators, slots, window):
    all_boxes, width = sources.shape
    boxes = 2 * (all_boxes // slots)
    kinds, _, dirs = translators.shape
    out_shape = (
        jax.ShapeDtypeStruct((table_rows(kinds), boxes * window), BF),
        jax.ShapeDtypeStruct((dirs, 2 * boxes, window), BF),
    )
    scratch = [
        pltpu.VMEM(sources.shape, I32),
        pltpu.VMEM(sources.shape, I32),
        pltpu.VMEM(translators.shape, BF),
        pltpu.VMEM((2 * boxes, round_up(width, LANES)), I32),
        pltpu.VMEM((2 * dirs, table_rows(kinds)), BF),
        pltpu.VMEM((window // LANES, dirs * (2 * boxes + 1), LANES), F32),
    ]
    return pl.pallas_call(
        functools.partial(first_kernel, slots),
        out_shape=out_shape,
        in_specs=[SMEM] + [pl.BlockSpec(memory_space=pltpu.HBM)] * 3,
        out_specs=(VMEM, VMEM),
        scratch_shapes=scratch + [pltpu.SemaphoreType.DMA((3,))],
        compiler_params=grant(scratch, out_shape),
        cost_estimate=cost(1 << 30, 1 << 20),
        name="first",
    )(place, sources, operator_ids, translators)


def transfer_kernel(place_ref, counts_ref, mine_ref, other_ref, matrix_ref, low, high, table, wide):
    upper = place_ref[1] % 2 == 1

    @pl.when(upper)
    def _():
        low[...], high[...] = other_ref[...], mine_ref[...]

    @pl.when(jnp.logical_not(upper))
    def _():
        low[...], high[...] = mine_ref[...], other_ref[...]

    fill_matrix(low, high, counts_ref, matrix_ref, table, wide)


def transfer(place, counts, mine, other, boxes, window):
    _, _, dirs = mine.shape
    out_shape = jax.ShapeDtypeStruct((dirs, 2 * boxes, window), BF)
    scratch = [
        pltpu.VMEM(mine.shape, BF),
        pltpu.VMEM(mine.shape, BF),
        pltpu.VMEM((2 * dirs, counts.shape[0]), BF),
        pltpu.VMEM((window // LANES, dirs * (2 * boxes + 1), LANES), F32),
    ]
    return pl.pallas_call(
        transfer_kernel,
        out_shape=out_shape,
        in_specs=[SMEM] + [VMEM] * 3,
        out_specs=VMEM,
        scratch_shapes=scratch,
        compiler_params=grant(scratch, [out_shape, counts, mine, other]),
        cost_estimate=cost(1 << 30, 1 << 20),
        name="transfer",
    )(place, counts, mine, other)


def rotated(box):
    half = box.shape[1] // 2
    re, im = box[:, :half], box[:, half:]
    return jnp.concatenate(
        [jnp.concatenate([re, -im], axis=1), jnp.concatenate([im, re], axis=1)], axis=0
    )


def radiate(forward, box_refs, incid, out, stride):
    dirs = forward.shape[0]
    at = 0
    for ref in box_refs:
        for row in range(0, ref.shape[0] // incid * incid, 2 * incid):
            both = [rotated(ref[i : i + incid, :]) for i in (row, row + incid)]
            field = dot(forward[...], jnp.concatenate(both, axis=0), NT)
            out[pl.ds(at, dirs, stride=stride), :] = field[:, : 2 * incid]
            out[pl.ds(at + 1, dirs, stride=stride), :] = field[:, 2 * incid :]
            at += 2


def early_kernel(parts, count, incid, *refs):
    forward_refs, refs = refs[1 : 1 + parts], refs[1 + parts :]
    box_refs, (pattern_ref, turned_ref, wide) = refs[:count], refs[count:]
    rows, boxes, _ = pattern_ref.shape
    dirs = rows // parts
    for j, ref in enumerate(forward_refs):
        flat = jnp.concatenate([ref[:, 0, :], ref[:, 1, :]], axis=1)
        turned_ref[j * dirs : (j + 1) * dirs, :] = flat
    radiate(turned_ref, box_refs, incid, wide, boxes + 1)

    def narrow(k):
        pattern_ref[k] = wide[pl.ds(k * (boxes + 1), boxes), :].astype(BF)

    unrolled(rows, 32, narrow)


def early_pattern(place, radiation, shards, slots, incid, dirs):
    boxes = sum(s.shape[0] // incid for s in shards)
    _, parts, unk = radiation.shape
    rows = len(slots) * dirs
    blocks = [
        pl.BlockSpec((dirs, parts, unk), lambda i, at, j=j: (at[0] ^ j, 0, 0)) for j in slots
    ]
    out_shape = (
        jax.ShapeDtypeStruct((rows, boxes, 2 * incid), BF),
        jax.ShapeDtypeStruct((rows, parts * unk), BF),
    )
    scratch = [pltpu.VMEM((rows * (boxes + 1), 2 * incid), F32)]
    return pl.pallas_call(
        functools.partial(early_kernel, len(slots), len(shards), incid),
        out_shape=out_shape,
        grid_spec=pltpu.PrefetchScalarGridSpec(
            num_scalar_prefetch=1,
            grid=(1,),
            in_specs=blocks + [VMEM] * len(shards),
            out_specs=(VMEM, VMEM),
            scratch_shapes=scratch,
        ),
        compiler_params=grant(scratch, out_shape, shards, [radiation]),
        cost_estimate=cost(4 << 30, 4 << 20),
        name="early",
    )(place, *[radiation] * len(slots), *shards)


def pattern_kernel(slots, count, incid, rim, place_ref, turned_ref, receive_ref, *refs):
    box_refs, (pattern_ref, folded_ref, wide, tails) = refs[:count], refs[count:]
    rows, boxes, _ = pattern_ref.shape
    dirs = rows // len(slots)
    radiate(turned_ref, box_refs, incid, wide, boxes + 1)

    def narrow(k):
        pattern_ref[k] = wide[pl.ds(k * (boxes + 1), boxes), :].astype(BF)

    unrolled(rows, 32, narrow)

    own_dir = place_ref[0]
    points = tails.shape[1] // 2
    total = receive_ref.shape[0]
    for j, ref in enumerate(box_refs):
        tails[j] = ref[ref.shape[0] - 2 * points :, :].astype(F32)
    lane = count_of((2 * points, LANES), 1)
    source = count_of((tails.shape[2], LANES), 0)
    target = count_of((tails.shape[2], LANES), 1)
    head = as_bf16((target < rim) & (source == target))
    tail = as_bf16((target >= rim) & (target < 2 * rim) & (source == target + dirs - 2 * rim))
    for at, j in enumerate(slots):
        holder = own_dir ^ j
        follows = own_dir ^ lax.rem(holder + 1, count)
        leads = own_dir ^ lax.rem(holder + count - 1, count)
        ends = dot(tails[follows].astype(BF), head, NN) + dot(tails[leads].astype(BF), tail, NN)
        here = tails[j][:, :dirs]
        spot = count_of((points, LANES), 1)
        spot = jnp.where(spot < rim, spot + dirs, spot - 2 * rim)
        spots = [here[:points].astype(I32) + count_of((points, dirs), 1)]
        spots.append(ends[:points].astype(I32) + spot)
        gains = [here[points:], ends[points:]]
        start = holder * dirs
        after = receive_ref[pl.ds(lax.rem(start + dirs, total), rim)]
        before = receive_ref[pl.ds(lax.rem(start + total - rim, total), rim)]
        tables = [receive_ref[pl.ds(start, dirs)], jnp.concatenate([after, before], axis=0)]
        folded = None
        for spot, gain, table in zip(spots, gains, tables):
            extent = spot.shape[1]
            own = count_of((dirs, extent), 0)
            spread = jnp.zeros((dirs, extent), F32)
            for p in range(points):
                spread += jnp.where(own == spot[p : p + 1, :], gain[p : p + 1, :], 0.0)
            flat = jnp.concatenate([table[:, 0, :], table[:, 1, :]], axis=1)
            if flat.shape[0] < extent:
                blank = jnp.zeros((extent - flat.shape[0], flat.shape[1]), BF)
                flat = jnp.concatenate([flat, blank], axis=0)
            part = dot(spread.astype(BF), flat, NN)
            folded = part if folded is None else folded + part
        folded_ref[at * dirs : (at + 1) * dirs, :] = folded.astype(BF)


def own_pattern(place, forward, receiving, shards, slots, incid, points):
    count = len(shards)
    boxes = sum(s.shape[0] // incid for s in shards)
    rows, width = forward.shape
    out_shape = (
        jax.ShapeDtypeStruct((rows, boxes, 2 * incid), BF),
        jax.ShapeDtypeStruct((rows, width), BF),
    )
    scratch = [
        pltpu.VMEM((rows * (boxes + 1), 2 * incid), F32),
        pltpu.VMEM((count, 2 * points, shards[0].shape[1]), F32),
    ]
    return pl.pallas_call(
        functools.partial(pattern_kernel, slots, count, incid, RIM),
        out_shape=out_shape,
        in_specs=[SMEM] + [VMEM] * (2 + count),
        out_specs=(VMEM, VMEM),
        scratch_shapes=scratch,
        compiler_params=grant(scratch, out_shape, shards, [forward, receiving]),
        cost_estimate=cost(4 << 30, 4 << 20),
        name="pattern",
    )(place, forward, receiving, *shards)


def receive(moved, folded, first, out_ref, stride):
    rows, half, unk = folded.shape[0], moved.shape[1] // 2, folded.shape[1] // 2
    count = out_ref.shape[0]
    step = 4 if count % 4 == 0 else 1
    for begin in range(0, count, step):
        fields = [
            moved[pl.ds(first + begin + i, rows, stride=stride), :].astype(BF) for i in range(step)
        ]
        every = dot(jnp.concatenate(fields, axis=1), folded[...], TN)
        for i in range(step):
            full = every[2 * half * i : 2 * half * (i + 1)]
            re = full[:half, :unk] - full[half:, unk:]
            im = full[:half, unk:] + full[half:, :unk]
            out_ref[begin + i] = jnp.concatenate([re, im], axis=1).astype(out_ref.dtype)


def field_kernel(slices, forward_ref, folded_ref, own_ref, early_ref, *refs):
    matrix_refs, refs = refs[:slices], refs[slices:]
    box_refs, (pair_ref, moved, near) = refs[:-3], refs[-3:]
    rows, own_boxes, width = own_ref.shape
    per, half, _ = pair_ref.shape
    boxes = 2 * per
    near_boxes = len(box_refs) * per
    radiate(forward_ref, box_refs, half, near, near_boxes + 1)
    sign = jnp.where(count_of((boxes, width), 1) < half, -1.0, 1.0).astype(F32)
    stride = boxes + 1
    dirs = rows // slices
    window = own_boxes + early_ref.shape[1] + near_boxes
    for at, matrix_ref in enumerate(matrix_refs):

        def translate(i, at=at, matrix_ref=matrix_ref):
            k = at * dirs + i
            around = near[pl.ds(k * (near_boxes + 1), near_boxes), :].astype(BF)
            fields = jnp.concatenate([own_ref[k], early_ref[k], around], axis=0)
            both = dot(matrix_ref[i][:, :window], fields, NN)
            turned = pltpu.roll(both[boxes:], half, 1)
            moved[pl.ds(k * stride, boxes), :] = both[:boxes] + sign * turned

        unrolled(dirs, 64, translate)

    receive(moved, folded_ref, per, pair_ref, stride)


def translate_field(forward, folded, own, early, matrices, near, kind):
    rows, _, width = own.shape
    per = matrices[0].shape[1] // 4
    shape = (per, width // 2, folded.shape[1])
    out_shape = (
        jax.ShapeDtypeStruct(shape, kind),
        jax.ShapeDtypeStruct((rows * (2 * per + 1), width), F32),
    )
    scratch = [pltpu.VMEM((rows * (len(near) * per + 1), width), F32)]
    return pl.pallas_call(
        functools.partial(field_kernel, len(matrices)),
        out_shape=out_shape,
        in_specs=[VMEM] * (4 + len(matrices) + len(near)),
        out_specs=(VMEM, VMEM),
        scratch_shapes=scratch,
        compiler_params=grant(scratch, out_shape, [forward, folded, own, early], matrices, near),
        cost_estimate=cost(4 << 30, 16 << 20),
        name="field",
    )(forward, folded, own, early, *matrices, *near)


def finish_kernel(folded_ref, moved_ref, out_ref):
    receive(moved_ref, folded_ref, 0, out_ref, 2 * out_ref.shape[0] + 1)


def finish(folded, moved, shape):
    out_shape = jax.ShapeDtypeStruct(shape, F32)
    return pl.pallas_call(
        finish_kernel,
        out_shape=out_shape,
        in_specs=[VMEM, VMEM],
        out_specs=VMEM,
        compiler_params=grant([out_shape, folded, moved]),
        cost_estimate=cost(1 << 28, 1 << 20),
        name="finish",
    )(folded, moved)


def mask_rows(values, live_counts):
    column = jnp.arange(values.shape[-1], dtype=I32) % (values.shape[-1] // 2)
    keep = column[None, None, :] < live_counts[:, None, None]
    return jnp.where(keep, values, jnp.zeros_like(values))


def body(
    currents,
    live_counts,
    radiation,
    sources,
    operator_ids,
    translators,
    stencil,
    stencil_weights,
    receiving,
):
    n_dir, n_grp = lax.axis_size("dir"), lax.axis_size("grp")
    _, _, dirs = translators.shape
    per, incid, _ = currents.shape
    points = stencil.shape[1]
    window = round_up((2 * n_dir + 2) * per, LANES)
    place = jnp.stack([lax.axis_index("dir"), lax.axis_index("grp")]).astype(I32)

    def swap(values, bit):
        return lax.ppermute(values, "dir", [(i, i ^ bit) for i in range(n_dir)])

    def gather(values, last):
        slots = {0: values}
        bit = n_dir // 2
        while bit >= last:
            for j in sorted(slots):
                slots[j + bit] = swap(slots[j], bit)
            bit //= 2
        return [slots[j] for j in sorted(slots)]

    def across(values, step_of):
        pairs = []
        for g in range(n_grp):
            for d in range(n_dir):
                to = g + step_of(d, g)
                if 0 <= to < n_grp:
                    pairs.append((g * n_dir + d, to * n_dir + d))
        return lax.ppermute(values, ("grp", "dir"), pairs)

    shard, part = prepare(
        live_counts, stencil.T, stencil_weights.T, currents, translators, radiation.shape[0]
    )
    shards = gather(shard, 1)
    near = [across(shards[j], lambda d, g, j=j: 1 if d ^ j > d else -1) for j in range(2, n_dir)]
    next_to = []
    for j in range(2):
        next_to.append(across(shards[j], lambda d, g: 1 if g % 2 else -1))
        next_to.append(across(shards[j], lambda d, g: -1 if g % 2 else 1))
    counts, matrix = first_transfer(
        place, sources, operator_ids, translators, n_dir, window
    )
    matrices = [matrix]
    for j, mine in enumerate(gather(part, 2)[1:], 1):
        other = across(mine, lambda d, g: -1 if g % 2 else 1)
        matrices.append(transfer(place, counts, mine, other, 2 * per, window))
    bulk = dirs * ((n_dir + 4) * per + 1) * LANES * 4
    slices = len(matrices)
    size = max(n for n in range(1, slices + 1) if slices % n == 0 and (n == 1 or n * bulk <= 24 << 20))
    sums = None
    for first in range(0, slices, size):
        slots = [2 * j for j in range(first, first + size)]
        early, forward = early_pattern(place, radiation, next_to, slots, incid, dirs)
        own, folded = own_pattern(place, forward, receiving, shards, slots, incid, points)
        kind = BF if size == slices else F32
        pair, moved = translate_field(
            forward, folded, own, early, matrices[first : first + size], near, kind
        )
        product = [finish(folded, moved, pair.shape), pair]
        sums = product if sums is None else [a + b for a, b in zip(sums, product)]
    total = sums[0] + swap(sums[1].astype(BF), 1).astype(F32)
    return mask_rows(total, live_counts)


def solution(mesh):
    placed = (
        P(("grp", "dir"), None, None),
        P(("grp", "dir")),
        P(),
        P("grp", None),
        P("grp", None),
        P(None, None, "dir"),
        P("dir", None),
        P("dir", None),
        P(),
    )
    return jax.shard_map(
        body,
        mesh=mesh,
        in_specs=placed,
        out_specs=P(("grp", "dir"), None, None),
        check_vma=False,
    )
```

```python
import functools
import math

import jax
import jax.numpy as jnp
from jax import lax
from jax.experimental import pallas as pl
from jax.experimental.pallas import tpu as pltpu
from jax.sharding import PartitionSpec as P


RIM = 8
LANES = 128
BF = jnp.bfloat16
F32 = jnp.float32
I32 = jnp.int32
NT = (((1,), (1,)), ((), ()))
TN = (((0,), (0,)), ((), ()))
NN = (((1,), (0,)), ((), ()))
VMEM = pl.BlockSpec(memory_space=pltpu.VMEM)
SMEM = pl.BlockSpec(memory_space=pltpu.SMEM)


def round_up(value, unit):
    return -(-value // unit) * unit


def half_of(kinds):
    return (kinds + 1) // 2


def table_rows(kinds):
    return round_up(2 * round_up(half_of(kinds), 16), LANES)


def dot(a, b, dims):
    return lax.dot_general(a, b, dims, preferred_element_type=F32)


def cost(flops, nbytes):
    return pl.CostEstimate(flops=int(flops), bytes_accessed=int(nbytes), transcendentals=0)


def grant(*groups):
    size = 4 << 20
    for group in groups:
        for item in group:
            size += math.prod(item.shape) * jnp.dtype(item.dtype).itemsize
    return pltpu.CompilerParams(vmem_limit_bytes=min(size, 60 * 1024 * 1024))


def count_of(shape, axis):
    return lax.broadcasted_iota(I32, shape, axis)


def as_bf16(mask):
    return mask.astype(F32).astype(BF)


def unrolled(trips, most, step):
    size = next(n for n in range(min(most, trips), 0, -1) if trips % n == 0)

    def block(i, carry):
        for j in range(size):
            step(i * size + j)
        return carry

    lax.fori_loop(0, trips // size, block, 0)


def prepare_kernel(all_dirs, live_ref, stencil_ref, weight_ref, box_ref, table_ref, out_ref, half_ref, sem):
    boxes, incid, width = box_ref.shape
    points, dirs = stencil_ref.shape
    half = half_ref.shape[0]
    first = lax.rem(lax.axis_index("grp"), 2) * (table_ref.shape[0] - half)
    fetch = pltpu.make_async_copy(table_ref.at[pl.ds(first, half)], half_ref, sem)
    fetch.start()
    unk = count_of((incid, width), 1)
    unk = jnp.where(unk < width // 2, unk, unk - width // 2)
    for b in range(boxes):
        kept = jnp.where(unk < live_ref[b], box_ref[b].astype(F32), 0.0)
        out_ref[b * incid : (b + 1) * incid, :] = kept.astype(BF)
    away = stencil_ref[...] - (count_of((points, dirs), 1) + lax.axis_index("dir") * dirs)
    away = jnp.where(away > all_dirs // 2, away - all_dirs, away)
    away = jnp.where(away < -(all_dirs // 2), away + all_dirs, away)
    rows = jnp.concatenate([away.astype(F32), weight_ref[...].astype(F32)], axis=0)
    if dirs < width:
        rows = jnp.concatenate([rows, jnp.zeros((2 * points, width - dirs), F32)], axis=1)
    out_ref[boxes * incid :, :] = rows.astype(BF)
    fetch.wait()


def prepare(live_counts, stencil, weights, currents, translators, all_dirs):
    boxes, incid, width = currents.shape
    points, dirs = stencil.shape
    kinds, parts, _ = translators.shape
    return pl.pallas_call(
        functools.partial(prepare_kernel, all_dirs),
        out_shape=(
            jax.ShapeDtypeStruct((boxes * incid + 2 * points, width), BF),
            jax.ShapeDtypeStruct((half_of(kinds), parts, dirs), BF),
        ),
        in_specs=[SMEM, VMEM, VMEM, VMEM, pl.BlockSpec(memory_space=pl.ANY)],
        out_specs=(VMEM, VMEM),
        scratch_shapes=[pltpu.SemaphoreType.DMA],
        cost_estimate=cost(1 << 20, 1 << 20),
        name="prepare",
    )(live_counts, stencil, weights, currents, translators)


def count_entries(slots, kinds, window, place_ref, source_ref, kind_ref, counts_ref, lists):
    all_boxes, width = source_ref.shape
    per = all_boxes // slots
    own_dir, own_group = place_ref[0], place_ref[1]
    half = half_of(kinds)
    lists[...] = jnp.full(lists.shape, -1, I32)
    for i in range(2):
        first = pl.multiple_of((own_dir ^ i) * per, 8)
        local = source_ref[pl.ds(first, per), :] - (own_group - 1) * all_boxes
        group = (local >= all_boxes).astype(I32) + (local >= 2 * all_boxes).astype(I32)
        inside = local - group * all_boxes
        holder = jnp.zeros_like(inside)
        for j in range(1, slots):
            holder += (inside >= j * per).astype(I32)
        slot = own_dir ^ holder
        side = jnp.where(group == jnp.where(own_group % 2 == 0, 2, 0), 1, 0)
        around = jnp.where(slot < 2, slots + 2 * slot + side, slots + 2 + slot)
        slot = jnp.where(group == 1, slot, around)
        lists[i * per : (i + 1) * per, :width] = slot * per + inside - holder * per
        kind = kind_ref[pl.ds(first, per), :]
        upper = kind - (kinds - half) + round_up(half, 16)
        kind = jnp.where(kind < half, kind, upper)
        lists[(2 + i) * per : (3 + i) * per, :width] = kind
    lanes = lists.shape[1]
    used = 2 * round_up(half, 16)
    if used < counts_ref.shape[0]:
        rest = (counts_ref.shape[0] - used, counts_ref.shape[1])
        counts_ref[used:, :] = jnp.zeros(rest, BF)
    for i in range(2 * per):
        hit_kind = count_of((used, lanes), 0) == lists[2 * per + i : 2 * per + i + 1, :]
        hit_source = count_of((window, lanes), 0) == lists[i : i + 1, :]
        counts = dot(as_bf16(hit_kind), as_bf16(hit_source), NT)
        counts_ref[:used, i * window : (i + 1) * window] = counts.astype(BF)


def fill_matrix(low, high, counts_ref, matrix_ref, table, wide):
    dirs, rows, window = matrix_ref.shape
    boxes, per = rows // 2, rows // 4
    half = low.shape[0]
    gap = round_up(half, 16) - half
    for c in range(2):
        fill = jnp.zeros((table.shape[1] - 2 * half - gap, dirs), BF)
        blank = jnp.zeros((gap, dirs), BF)
        part = jnp.concatenate([low[:, c, :], blank, high[:, c, :], fill], axis=0)
        table[c * dirs : (c + 1) * dirs, :] = part.T
    for at in range(0, boxes, 2):
        entries = dot(table[...], counts_ref[:, at * window : (at + 2) * window], NN)
        for i in range(2):
            for c in range(window // LANES):
                part = entries[:, i * window + c * LANES : i * window + (c + 1) * LANES]
                spot = at + i + (at + i) // per * per
                wide[c, pl.ds(spot, dirs, stride=rows + 1), :] = part[:dirs]
                wide[c, pl.ds(spot + per, dirs, stride=rows + 1), :] = part[dirs:]

    def narrow(k):
        for c in range(window // LANES):
            part = wide[c, pl.ds(k * (rows + 1), rows), :]
            matrix_ref[k, :, c * LANES : (c + 1) * LANES] = part.astype(BF)

    unrolled(dirs, 64, narrow)


def first_kernel(slots, place_ref, source_hbm, kind_hbm, table_hbm, counts_ref, matrix_ref, *scratch):
    source_ref, kind_ref, table_ref, lists, table, wide, sems = scratch
    window = matrix_ref.shape[2]
    kinds = table_ref.shape[0]
    copies = [
        pltpu.make_async_copy(source_hbm, source_ref, sems.at[0]),
        pltpu.make_async_copy(kind_hbm, kind_ref, sems.at[1]),
        pltpu.make_async_copy(table_hbm, table_ref, sems.at[2]),
    ]
    for copy in copies:
        copy.start()
    copies[0].wait()
    copies[1].wait()
    count_entries(slots, kinds, window, place_ref, source_ref, kind_ref, counts_ref, lists)
    copies[2].wait()
    half = half_of(kinds)
    low, high = table_ref.at[pl.ds(0, half)], table_ref.at[pl.ds(kinds - half, half)]
    fill_matrix(low, high, counts_ref, matrix_ref, table, wide)


def first_transfer(place, sources, operator_ids, translators, slots, window):
    all_boxes, width = sources.shape
    boxes = 2 * (all_boxes // slots)
    kinds, _, dirs = translators.shape
    out_shape = (
        jax.ShapeDtypeStruct((table_rows(kinds), boxes * window), BF),
        jax.ShapeDtypeStruct((dirs, 2 * boxes, window), BF),
    )
    scratch = [
        pltpu.VMEM(sources.shape, I32),
        pltpu.VMEM(sources.shape, I32),
        pltpu.VMEM(translators.shape, BF),
        pltpu.VMEM((2 * boxes, round_up(width, LANES)), I32),
        pltpu.VMEM((2 * dirs, table_rows(kinds)), BF),
        pltpu.VMEM((window // LANES, dirs * (2 * boxes + 1), LANES), F32),
    ]
    return pl.pallas_call(
        functools.partial(first_kernel, slots),
        out_shape=out_shape,
        in_specs=[SMEM] + [pl.BlockSpec(memory_space=pltpu.HBM)] * 3,
        out_specs=(VMEM, VMEM),
        scratch_shapes=scratch + [pltpu.SemaphoreType.DMA((3,))],
        compiler_params=grant(scratch, out_shape),
        cost_estimate=cost(1 << 30, 1 << 20),
        name="first",
    )(place, sources, operator_ids, translators)


def transfer_kernel(place_ref, counts_ref, mine_ref, other_ref, matrix_ref, low, high, table, wide):
    upper = place_ref[1] % 2 == 1

    @pl.when(upper)
    def _():
        low[...], high[...] = other_ref[...], mine_ref[...]

    @pl.when(jnp.logical_not(upper))
    def _():
        low[...], high[...] = mine_ref[...], other_ref[...]

    fill_matrix(low, high, counts_ref, matrix_ref, table, wide)


def transfer(place, counts, mine, other, boxes, window):
    _, _, dirs = mine.shape
    out_shape = jax.ShapeDtypeStruct((dirs, 2 * boxes, window), BF)
    scratch = [
        pltpu.VMEM(mine.shape, BF),
        pltpu.VMEM(mine.shape, BF),
        pltpu.VMEM((2 * dirs, counts.shape[0]), BF),
        pltpu.VMEM((window // LANES, dirs * (2 * boxes + 1), LANES), F32),
    ]
    return pl.pallas_call(
        transfer_kernel,
        out_shape=out_shape,
        in_specs=[SMEM] + [VMEM] * 3,
        out_specs=VMEM,
        scratch_shapes=scratch,
        compiler_params=grant(scratch, [out_shape, counts, mine, other]),
        cost_estimate=cost(1 << 30, 1 << 20),
        name="transfer",
    )(place, counts, mine, other)


def rotated(box):
    half = box.shape[1] // 2
    re, im = box[:, :half], box[:, half:]
    return jnp.concatenate(
        [jnp.concatenate([re, -im], axis=1), jnp.concatenate([im, re], axis=1)], axis=0
    )


def radiate(forward, box_refs, incid, out, stride):
    dirs = forward.shape[0]
    at = 0
    for ref in box_refs:
        for row in range(0, ref.shape[0] // incid * incid, 2 * incid):
            both = [rotated(ref[i : i + incid, :]) for i in (row, row + incid)]
            field = dot(forward[...], jnp.concatenate(both, axis=0), NT)
            out[pl.ds(at, dirs, stride=stride), :] = field[:, : 2 * incid]
            out[pl.ds(at + 1, dirs, stride=stride), :] = field[:, 2 * incid :]
            at += 2


def early_kernel(parts, count, incid, *refs):
    forward_refs, refs = refs[1 : 1 + parts], refs[1 + parts :]
    box_refs, (pattern_ref, turned_ref, wide) = refs[:count], refs[count:]
    rows, boxes, _ = pattern_ref.shape
    dirs = rows // parts
    for j, ref in enumerate(forward_refs):
        flat = jnp.concatenate([ref[:, 0, :], ref[:, 1, :]], axis=1)
        turned_ref[j * dirs : (j + 1) * dirs, :] = flat
    radiate(turned_ref, box_refs, incid, wide, boxes + 1)

    def narrow(k):
        pattern_ref[k] = wide[pl.ds(k * (boxes + 1), boxes), :].astype(BF)

    unrolled(rows, 32, narrow)


def early_pattern(place, radiation, shards, slots, incid, dirs):
    boxes = sum(s.shape[0] // incid for s in shards)
    _, parts, unk = radiation.shape
    rows = len(slots) * dirs
    blocks = [
        pl.BlockSpec((dirs, parts, unk), lambda i, at, j=j: (at[0] ^ j, 0, 0)) for j in slots
    ]
    out_shape = (
        jax.ShapeDtypeStruct((rows, boxes, 2 * incid), BF),
        jax.ShapeDtypeStruct((rows, parts * unk), BF),
    )
    scratch = [pltpu.VMEM((rows * (boxes + 1), 2 * incid), F32)]
    return pl.pallas_call(
        functools.partial(early_kernel, len(slots), len(shards), incid),
        out_shape=out_shape,
        grid_spec=pltpu.PrefetchScalarGridSpec(
            num_scalar_prefetch=1,
            grid=(1,),
            in_specs=blocks + [VMEM] * len(shards),
            out_specs=(VMEM, VMEM),
            scratch_shapes=scratch,
        ),
        compiler_params=grant(scratch, out_shape, shards, [radiation]),
        cost_estimate=cost(4 << 30, 4 << 20),
        name="early",
    )(place, *[radiation] * len(slots), *shards)


def pattern_kernel(slots, count, incid, rim, place_ref, turned_ref, receive_ref, *refs):
    box_refs, (pattern_ref, folded_ref, wide, tails) = refs[:count], refs[count:]
    rows, boxes, _ = pattern_ref.shape
    dirs = rows // len(slots)
    radiate(turned_ref, box_refs, incid, wide, boxes + 1)

    def narrow(k):
        pattern_ref[k] = wide[pl.ds(k * (boxes + 1), boxes), :].astype(BF)

    unrolled(rows, 32, narrow)

    own_dir = place_ref[0]
    points = tails.shape[1] // 2
    total = receive_ref.shape[0]
    for j, ref in enumerate(box_refs):
        tails[j] = ref[ref.shape[0] - 2 * points :, :].astype(F32)
    lane = count_of((2 * points, LANES), 1)
    source = count_of((tails.shape[2], LANES), 0)
    target = count_of((tails.shape[2], LANES), 1)
    head = as_bf16((target < rim) & (source == target))
    tail = as_bf16((target >= rim) & (target < 2 * rim) & (source == target + dirs - 2 * rim))
    for at, j in enumerate(slots):
        holder = own_dir ^ j
        follows = own_dir ^ lax.rem(holder + 1, count)
        leads = own_dir ^ lax.rem(holder + count - 1, count)
        ends = dot(tails[follows].astype(BF), head, NN) + dot(tails[leads].astype(BF), tail, NN)
        here = tails[j][:, :dirs]
        spot = count_of((points, LANES), 1)
        spot = jnp.where(spot < rim, spot + dirs, spot - 2 * rim)
        spots = [here[:points].astype(I32) + count_of((points, dirs), 1)]
        spots.append(ends[:points].astype(I32) + spot)
        gains = [here[points:], ends[points:]]
        start = holder * dirs
        after = receive_ref[pl.ds(lax.rem(start + dirs, total), rim)]
        before = receive_ref[pl.ds(lax.rem(start + total - rim, total), rim)]
        tables = [receive_ref[pl.ds(start, dirs)], jnp.concatenate([after, before], axis=0)]
        folded = None
        for spot, gain, table in zip(spots, gains, tables):
            extent = spot.shape[1]
            own = count_of((dirs, extent), 0)
            spread = jnp.zeros((dirs, extent), F32)
            for p in range(points):
                spread += jnp.where(own == spot[p : p + 1, :], gain[p : p + 1, :], 0.0)
            flat = jnp.concatenate([table[:, 0, :], table[:, 1, :]], axis=1)
            if flat.shape[0] < extent:
                blank = jnp.zeros((extent - flat.shape[0], flat.shape[1]), BF)
                flat = jnp.concatenate([flat, blank], axis=0)
            part = dot(spread.astype(BF), flat, NN)
            folded = part if folded is None else folded + part
        folded_ref[at * dirs : (at + 1) * dirs, :] = folded.astype(BF)


def own_pattern(place, forward, receiving, shards, slots, incid, points):
    count = len(shards)
    boxes = sum(s.shape[0] // incid for s in shards)
    rows, width = forward.shape
    out_shape = (
        jax.ShapeDtypeStruct((rows, boxes, 2 * incid), BF),
        jax.ShapeDtypeStruct((rows, width), BF),
    )
    scratch = [
        pltpu.VMEM((rows * (boxes + 1), 2 * incid), F32),
        pltpu.VMEM((count, 2 * points, shards[0].shape[1]), F32),
    ]
    return pl.pallas_call(
        functools.partial(pattern_kernel, slots, count, incid, RIM),
        out_shape=out_shape,
        in_specs=[SMEM] + [VMEM] * (2 + count),
        out_specs=(VMEM, VMEM),
        scratch_shapes=scratch,
        compiler_params=grant(scratch, out_shape, shards, [forward, receiving]),
        cost_estimate=cost(4 << 30, 4 << 20),
        name="pattern",
    )(place, forward, receiving, *shards)


def receive(moved, folded, first, out_ref, stride):
    rows, half, unk = folded.shape[0], moved.shape[1] // 2, folded.shape[1] // 2
    count = out_ref.shape[0]
    step = 4 if count % 4 == 0 else 1
    for begin in range(0, count, step):
        fields = [
            moved[pl.ds(first + begin + i, rows, stride=stride), :].astype(BF) for i in range(step)
        ]
        every = dot(jnp.concatenate(fields, axis=1), folded[...], TN)
        for i in range(step):
            full = every[2 * half * i : 2 * half * (i + 1)]
            re = full[:half, :unk] - full[half:, unk:]
            im = full[:half, unk:] + full[half:, :unk]
            out_ref[begin + i] = jnp.concatenate([re, im], axis=1).astype(out_ref.dtype)


def translate(part, matrix_refs, own_ref, early_ref, near, moved):
    rows, own_boxes, width = own_ref.shape
    dirs, lines, _ = matrix_refs[0].shape
    per, half = lines // 4, width // 2
    near_boxes = near.shape[0] // rows - 1
    window = own_boxes + early_ref.shape[1] + near_boxes
    sign = jnp.where(count_of((per, width), 1) < half, -1.0, 1.0).astype(F32)
    for at, matrix_ref in enumerate(matrix_refs):

        def two(i, at=at, matrix_ref=matrix_ref):
            fields, weights = [], []
            for j in (2 * i, 2 * i + 1):
                k = at * dirs + j
                around = near[pl.ds(k * (near_boxes + 1), near_boxes), :].astype(BF)
                fields.append(jnp.concatenate([own_ref[k], early_ref[k], around], axis=0))
                weights.append(matrix_ref[j][2 * per * part : 2 * per * (part + 1), :window])
            both = dot(jnp.concatenate(weights, axis=0), jnp.concatenate(fields, axis=1), NN)
            for j in range(2):
                each = both[2 * per * j : 2 * per * (j + 1), width * j : width * (j + 1)]
                turned = pltpu.roll(each[per:], half, 1)
                begin = (at * dirs + 2 * i + j) * (per + 1)
                moved[pl.ds(begin, per), :] = each[:per] + sign * turned

        unrolled(dirs // 2, 32, two)


def field_kernel(slices, forward_ref, folded_ref, own_ref, early_ref, *refs):
    matrix_refs, refs = refs[:slices], refs[slices:]
    box_refs, (pair_ref, near, moved) = refs[:-3], refs[-3:]
    per, half, _ = pair_ref.shape
    radiate(forward_ref, box_refs, half, near, len(box_refs) * per + 1)
    translate(1, matrix_refs, own_ref, early_ref, near, moved)
    receive(moved, folded_ref, 0, pair_ref, per + 1)


def translate_field(forward, folded, own, early, matrices, near, kind):
    rows, _, width = own.shape
    per = matrices[0].shape[1] // 4
    shape = (per, width // 2, folded.shape[1])
    out_shape = (
        jax.ShapeDtypeStruct(shape, kind),
        jax.ShapeDtypeStruct((rows * (len(near) * per + 1), width), F32),
    )
    scratch = [pltpu.VMEM((rows * (per + 1), width), F32)]
    return pl.pallas_call(
        functools.partial(field_kernel, len(matrices)),
        out_shape=out_shape,
        in_specs=[VMEM] * (4 + len(matrices) + len(near)),
        out_specs=(VMEM, VMEM),
        scratch_shapes=scratch,
        compiler_params=grant(scratch, out_shape, [forward, folded, own, early], matrices, near),
        cost_estimate=cost(4 << 30, 16 << 20),
        name="field",
    )(forward, folded, own, early, *matrices, *near)


def finish_kernel(slices, folded_ref, own_ref, early_ref, near_ref, *refs):
    matrix_refs, (out_ref, moved) = refs[:slices], refs[slices:]
    translate(0, matrix_refs, own_ref, early_ref, near_ref, moved)
    receive(moved, folded_ref, 0, out_ref, out_ref.shape[0] + 1)


def finish(folded, own, early, around, matrices, shape):
    out_shape = jax.ShapeDtypeStruct(shape, F32)
    rows, _, width = own.shape
    scratch = [pltpu.VMEM((rows * (shape[0] + 1), width), F32)]
    return pl.pallas_call(
        functools.partial(finish_kernel, len(matrices)),
        out_shape=out_shape,
        in_specs=[VMEM] * (4 + len(matrices)),
        out_specs=VMEM,
        scratch_shapes=scratch,
        compiler_params=grant(scratch, [out_shape, folded, own, early, around], matrices),
        cost_estimate=cost(2 << 30, 8 << 20),
        name="finish",
    )(folded, own, early, around, *matrices)


def mask_rows(values, live_counts):
    column = jnp.arange(values.shape[-1], dtype=I32) % (values.shape[-1] // 2)
    keep = column[None, None, :] < live_counts[:, None, None]
    return jnp.where(keep, values, jnp.zeros_like(values))


def body(
    currents,
    live_counts,
    radiation,
    sources,
    operator_ids,
    translators,
    stencil,
    stencil_weights,
    receiving,
):
    n_dir, n_grp = lax.axis_size("dir"), lax.axis_size("grp")
    _, _, dirs = translators.shape
    per, incid, _ = currents.shape
    points = stencil.shape[1]
    window = round_up((2 * n_dir + 2) * per, LANES)
    place = jnp.stack([lax.axis_index("dir"), lax.axis_index("grp")]).astype(I32)

    def swap(values, bit):
        return lax.ppermute(values, "dir", [(i, i ^ bit) for i in range(n_dir)])

    def gather(values, last):
        slots = {0: values}
        bit = n_dir // 2
        while bit >= last:
            for j in sorted(slots):
                slots[j + bit] = swap(slots[j], bit)
            bit //= 2
        return [slots[j] for j in sorted(slots)]

    def across(values, step_of):
        pairs = []
        for g in range(n_grp):
            for d in range(n_dir):
                to = g + step_of(d, g)
                if 0 <= to < n_grp:
                    pairs.append((g * n_dir + d, to * n_dir + d))
        return lax.ppermute(values, ("grp", "dir"), pairs)

    shard, part = prepare(
        live_counts, stencil.T, stencil_weights.T, currents, translators, radiation.shape[0]
    )
    shards = gather(shard, 1)
    near = [across(shards[j], lambda d, g, j=j: 1 if d ^ j > d else -1) for j in range(2, n_dir)]
    next_to = []
    for j in range(2):
        next_to.append(across(shards[j], lambda d, g: 1 if g % 2 else -1))
        next_to.append(across(shards[j], lambda d, g: -1 if g % 2 else 1))
    counts, matrix = first_transfer(
        place, sources, operator_ids, translators, n_dir, window
    )
    matrices = [matrix]
    for j, mine in enumerate(gather(part, 2)[1:], 1):
        other = across(mine, lambda d, g: -1 if g % 2 else 1)
        matrices.append(transfer(place, counts, mine, other, 2 * per, window))
    bulk = dirs * ((n_dir + 4) * per + 1) * LANES * 4
    slices = len(matrices)
    size = max(n for n in range(1, slices + 1) if slices % n == 0 and (n == 1 or n * bulk <= 20 << 20))
    sums = None
    for first in range(0, slices, size):
        slots = [2 * j for j in range(first, first + size)]
        early, forward = early_pattern(place, radiation, next_to, slots, incid, dirs)
        own, folded = own_pattern(place, forward, receiving, shards, slots, incid, points)
        kind = BF if size == slices else F32
        pair, around = translate_field(
            forward, folded, own, early, matrices[first : first + size], near, kind
        )
        mine = finish(
            folded, own, early, around, matrices[first : first + size], pair.shape
        )
        product = [mine, pair]
        sums = product if sums is None else [a + b for a, b in zip(sums, product)]
    total = sums[0] + swap(sums[1].astype(BF), 1).astype(F32)
    return mask_rows(total, live_counts)


def solution(mesh):
    placed = (
        P(("grp", "dir"), None, None),
        P(("grp", "dir")),
        P(),
        P("grp", None),
        P("grp", None),
        P(None, None, "dir"),
        P("dir", None),
        P("dir", None),
        P(),
    )
    return jax.shard_map(
        body,
        mesh=mesh,
        in_specs=placed,
        out_specs=P(("grp", "dir"), None, None),
        check_vma=False,
    )
```

```python
import functools
import math

import jax
import jax.numpy as jnp
from jax import lax
from jax.experimental import pallas as pl
from jax.experimental.pallas import tpu as pltpu
from jax.sharding import PartitionSpec as P


RIM = 8
LANES = 128
BF = jnp.bfloat16
F32 = jnp.float32
I32 = jnp.int32
NT = (((1,), (1,)), ((), ()))
TN = (((0,), (0,)), ((), ()))
NN = (((1,), (0,)), ((), ()))
VMEM = pl.BlockSpec(memory_space=pltpu.VMEM)
SMEM = pl.BlockSpec(memory_space=pltpu.SMEM)


def round_up(value, unit):
    return -(-value // unit) * unit


def padded_rows(rows, boxes):
    return rows * (boxes + 1) + round_up(boxes + 1, 8)


def half_of(kinds):
    return (kinds + 1) // 2


def table_rows(kinds):
    return round_up(2 * round_up(half_of(kinds), 16), LANES)


def dot(a, b, dims):
    return lax.dot_general(a, b, dims, preferred_element_type=F32)


def cost(flops, nbytes):
    return pl.CostEstimate(flops=int(flops), bytes_accessed=int(nbytes), transcendentals=0)


def grant(*groups):
    size = 4 << 20
    for group in groups:
        for item in group:
            size += math.prod(item.shape) * jnp.dtype(item.dtype).itemsize
    return pltpu.CompilerParams(vmem_limit_bytes=min(size, 60 * 1024 * 1024))


def count_of(shape, axis):
    return lax.broadcasted_iota(I32, shape, axis)


def as_bf16(mask):
    return mask.astype(F32).astype(BF)


def unrolled(trips, most, step):
    size = next(n for n in range(min(most, trips), 0, -1) if trips % n == 0)

    def block(i, carry):
        for j in range(size):
            step(i * size + j)
        return carry

    lax.fori_loop(0, trips // size, block, 0)


def prepare_kernel(all_dirs, live_ref, stencil_ref, weight_ref, box_ref, out_ref):
    boxes, incid, width = box_ref.shape
    points, dirs = stencil_ref.shape
    unk = count_of((incid, width), 1)
    unk = jnp.where(unk < width // 2, unk, unk - width // 2)
    for b in range(boxes):
        kept = jnp.where(unk < live_ref[b], box_ref[b].astype(F32), 0.0)
        out_ref[b * incid : (b + 1) * incid, :] = kept.astype(BF)
    away = stencil_ref[...] - (count_of((points, dirs), 1) + lax.axis_index("dir") * dirs)
    away = jnp.where(away > all_dirs // 2, away - all_dirs, away)
    away = jnp.where(away < -(all_dirs // 2), away + all_dirs, away)
    rows = jnp.concatenate([away.astype(F32), weight_ref[...].astype(F32)], axis=0)
    if dirs < width:
        rows = jnp.concatenate([rows, jnp.zeros((2 * points, width - dirs), F32)], axis=1)
    out_ref[boxes * incid :, :] = rows.astype(BF)


def prepare(live_counts, stencil, weights, currents, all_dirs):
    boxes, incid, width = currents.shape
    points, _ = stencil.shape
    return pl.pallas_call(
        functools.partial(prepare_kernel, all_dirs),
        out_shape=jax.ShapeDtypeStruct((boxes * incid + 2 * points, width), BF),
        in_specs=[SMEM, VMEM, VMEM, VMEM],
        out_specs=VMEM,
        cost_estimate=cost(1 << 20, 1 << 20),
        name="prepare",
    )(live_counts, stencil, weights, currents)


def count_entries(slots, kinds, window, place_ref, source_ref, kind_ref, counts_ref, lists):
    all_boxes, width = source_ref.shape
    per = all_boxes // slots
    own_dir, own_group = place_ref[0], place_ref[1]
    half = half_of(kinds)
    lists[...] = jnp.full(lists.shape, -1, I32)
    for i in range(2):
        first = pl.multiple_of((own_dir ^ i) * per, 8)
        local = source_ref[pl.ds(first, per), :] - (own_group - 1) * all_boxes
        group = (local >= all_boxes).astype(I32) + (local >= 2 * all_boxes).astype(I32)
        inside = local - group * all_boxes
        holder = jnp.zeros_like(inside)
        for j in range(1, slots):
            holder += (inside >= j * per).astype(I32)
        slot = own_dir ^ holder
        side = jnp.where(group == jnp.where(own_group % 2 == 0, 2, 0), 1, 0)
        around = jnp.where(slot < 2, slots + 2 * slot + side, slots + 2 + slot)
        slot = jnp.where(group == 1, slot, around)
        lists[i * per : (i + 1) * per, :width] = slot * per + inside - holder * per
        kind = kind_ref[pl.ds(first, per), :]
        upper = kind - (kinds - half) + round_up(half, 16)
        kind = jnp.where(kind < half, kind, upper)
        lists[(2 + i) * per : (3 + i) * per, :width] = kind
    lanes = lists.shape[1]
    used = 2 * round_up(half, 16)
    if used < counts_ref.shape[0]:
        rest = (counts_ref.shape[0] - used, counts_ref.shape[1])
        counts_ref[used:, :] = jnp.zeros(rest, BF)
    for i in range(2 * per):
        hit_kind = count_of((used, lanes), 0) == lists[2 * per + i : 2 * per + i + 1, :]
        hit_source = count_of((window, lanes), 0) == lists[i : i + 1, :]
        counts = dot(as_bf16(hit_kind), as_bf16(hit_source), NT)
        counts_ref[:used, i * window : (i + 1) * window] = counts.astype(BF)


def fill_matrix(low, high, counts_ref, matrix_ref, table, wide):
    dirs, rows, window = matrix_ref.shape
    boxes, per = rows // 2, rows // 4
    half = low.shape[0]
    gap = round_up(half, 16) - half
    for c in range(2):
        fill = jnp.zeros((table.shape[1] - 2 * half - gap, dirs), BF)
        blank = jnp.zeros((gap, dirs), BF)
        part = jnp.concatenate([low[:, c, :], blank, high[:, c, :], fill], axis=0)
        table[c * dirs : (c + 1) * dirs, :] = part.T
    for at in range(0, boxes, 2):
        entries = dot(table[...], counts_ref[:, at * window : (at + 2) * window], NN)
        for i in range(2):
            for c in range(window // LANES):
                part = entries[:, i * window + c * LANES : i * window + (c + 1) * LANES]
                spot = at + i + (at + i) // per * per
                wide[c, pl.ds(spot, dirs, stride=rows + 1), :] = part[:dirs]
                wide[c, pl.ds(spot + per, dirs, stride=rows + 1), :] = part[dirs:]

    def narrow(k):
        for c in range(window // LANES):
            part = wide[c, pl.ds(k * (rows + 1), rows), :]
            matrix_ref[k, :, c * LANES : (c + 1) * LANES] = part.astype(BF)

    unrolled(dirs, 64, narrow)


def first_kernel(
    slots, place_ref, source_hbm, kind_hbm, table_hbm, counts_ref, matrix_ref, half_ref, *scratch
):
    source_ref, kind_ref, table_ref, lists, table, wide, sems = scratch
    window = matrix_ref.shape[2]
    kinds = table_ref.shape[0]
    copies = [
        pltpu.make_async_copy(source_hbm, source_ref, sems.at[0]),
        pltpu.make_async_copy(kind_hbm, kind_ref, sems.at[1]),
        pltpu.make_async_copy(table_hbm, table_ref, sems.at[2]),
    ]
    for copy in copies:
        copy.start()
    copies[0].wait()
    copies[1].wait()
    count_entries(slots, kinds, window, place_ref, source_ref, kind_ref, counts_ref, lists)
    copies[2].wait()
    half = half_of(kinds)
    half_ref[...] = table_ref[pl.ds(lax.rem(place_ref[1], 2) * (kinds - half), half)]
    low, high = table_ref.at[pl.ds(0, half)], table_ref.at[pl.ds(kinds - half, half)]
    fill_matrix(low, high, counts_ref, matrix_ref, table, wide)


def first_transfer(place, sources, operator_ids, translators, slots, window):
    all_boxes, width = sources.shape
    boxes = 2 * (all_boxes // slots)
    kinds, _, dirs = translators.shape
    out_shape = (
        jax.ShapeDtypeStruct((table_rows(kinds), boxes * window), BF),
        jax.ShapeDtypeStruct((dirs, 2 * boxes, window), BF),
        jax.ShapeDtypeStruct((half_of(kinds), 2, dirs), BF),
    )
    scratch = [
        pltpu.VMEM(sources.shape, I32),
        pltpu.VMEM(sources.shape, I32),
        pltpu.VMEM(translators.shape, BF),
        pltpu.VMEM((2 * boxes, round_up(width, LANES)), I32),
        pltpu.VMEM((2 * dirs, table_rows(kinds)), BF),
        pltpu.VMEM((window // LANES, padded_rows(dirs, 2 * boxes), LANES), F32),
    ]
    return pl.pallas_call(
        functools.partial(first_kernel, slots),
        out_shape=out_shape,
        in_specs=[SMEM] + [pl.BlockSpec(memory_space=pltpu.HBM)] * 3,
        out_specs=(VMEM, VMEM, VMEM),
        scratch_shapes=scratch + [pltpu.SemaphoreType.DMA((3,))],
        compiler_params=grant(scratch, out_shape),
        cost_estimate=cost(1 << 30, 1 << 20),
        name="first",
    )(place, sources, operator_ids, translators)


def transfer_kernel(place_ref, counts_ref, mine_ref, other_ref, matrix_ref, low, high, table, wide):
    upper = place_ref[1] % 2 == 1

    @pl.when(upper)
    def _():
        low[...], high[...] = other_ref[...], mine_ref[...]

    @pl.when(jnp.logical_not(upper))
    def _():
        low[...], high[...] = mine_ref[...], other_ref[...]

    fill_matrix(low, high, counts_ref, matrix_ref, table, wide)


def transfer(place, counts, mine, other, boxes, window):
    _, _, dirs = mine.shape
    out_shape = jax.ShapeDtypeStruct((dirs, 2 * boxes, window), BF)
    scratch = [
        pltpu.VMEM(mine.shape, BF),
        pltpu.VMEM(mine.shape, BF),
        pltpu.VMEM((2 * dirs, counts.shape[0]), BF),
        pltpu.VMEM((window // LANES, padded_rows(dirs, 2 * boxes), LANES), F32),
    ]
    return pl.pallas_call(
        transfer_kernel,
        out_shape=out_shape,
        in_specs=[SMEM] + [VMEM] * 3,
        out_specs=VMEM,
        scratch_shapes=scratch,
        compiler_params=grant(scratch, [out_shape, counts, mine, other]),
        cost_estimate=cost(1 << 30, 1 << 20),
        name="transfer",
    )(place, counts, mine, other)


def rotated(box):
    half = box.shape[1] // 2
    re, im = box[:, :half], box[:, half:]
    return jnp.concatenate(
        [jnp.concatenate([re, -im], axis=1), jnp.concatenate([im, re], axis=1)], axis=0
    )


def radiate(forward, box_refs, incid, out, stride):
    dirs = forward.shape[0]
    at = 0
    for ref in box_refs:
        for row in range(0, ref.shape[0] // incid * incid, 2 * incid):
            both = [rotated(ref[i : i + incid, :]) for i in (row, row + incid)]
            field = dot(forward[...], jnp.concatenate(both, axis=0), NT)
            out[pl.ds(at, dirs, stride=stride), :] = field[:, : 2 * incid]
            out[pl.ds(at + 1, dirs, stride=stride), :] = field[:, 2 * incid :]
            at += 2


def early_kernel(parts, count, incid, *refs):
    forward_refs, refs = refs[1 : 1 + parts], refs[1 + parts :]
    box_refs, (pattern_ref, turned_ref, wide) = refs[:count], refs[count:]
    rows, boxes, _ = pattern_ref.shape
    dirs = rows // parts
    for j, ref in enumerate(forward_refs):
        flat = jnp.concatenate([ref[:, 0, :], ref[:, 1, :]], axis=1)
        turned_ref[j * dirs : (j + 1) * dirs, :] = flat
    radiate(turned_ref, box_refs, incid, wide, boxes + 1)

    def narrow(k):
        pattern_ref[k] = wide[pl.ds(k * (boxes + 1), boxes), :].astype(BF)

    unrolled(rows, 32, narrow)


def early_pattern(place, radiation, shards, slots, incid, dirs):
    boxes = sum(s.shape[0] // incid for s in shards)
    _, parts, unk = radiation.shape
    rows = len(slots) * dirs
    blocks = [
        pl.BlockSpec((dirs, parts, unk), lambda i, at, j=j: (at[0] ^ j, 0, 0)) for j in slots
    ]
    out_shape = (
        jax.ShapeDtypeStruct((rows, boxes, 2 * incid), BF),
        jax.ShapeDtypeStruct((rows, parts * unk), BF),
    )
    scratch = [pltpu.VMEM((padded_rows(rows, boxes), 2 * incid), F32)]
    return pl.pallas_call(
        functools.partial(early_kernel, len(slots), len(shards), incid),
        out_shape=out_shape,
        grid_spec=pltpu.PrefetchScalarGridSpec(
            num_scalar_prefetch=1,
            grid=(1,),
            in_specs=blocks + [VMEM] * len(shards),
            out_specs=(VMEM, VMEM),
            scratch_shapes=scratch,
        ),
        compiler_params=grant(scratch, out_shape, shards, [radiation]),
        cost_estimate=cost(4 << 30, 4 << 20),
        name="early",
    )(place, *[radiation] * len(slots), *shards)


def pattern_kernel(slots, count, incid, rim, place_ref, turned_ref, receive_ref, *refs):
    box_refs, (pattern_ref, folded_ref, wide, tails) = refs[:count], refs[count:]
    rows, boxes, _ = pattern_ref.shape
    dirs = rows // len(slots)
    radiate(turned_ref, box_refs, incid, wide, boxes + 1)

    def narrow(k):
        pattern_ref[k] = wide[pl.ds(k * (boxes + 1), boxes), :].astype(BF)

    unrolled(rows, 32, narrow)

    own_dir = place_ref[0]
    points = tails.shape[1] // 2
    total = receive_ref.shape[0]
    for j, ref in enumerate(box_refs):
        tails[j] = ref[ref.shape[0] - 2 * points :, :].astype(F32)
    lane = count_of((2 * points, LANES), 1)
    source = count_of((tails.shape[2], LANES), 0)
    target = count_of((tails.shape[2], LANES), 1)
    head = as_bf16((target < rim) & (source == target))
    tail = as_bf16((target >= rim) & (target < 2 * rim) & (source == target + dirs - 2 * rim))
    for at, j in enumerate(slots):
        holder = own_dir ^ j
        follows = own_dir ^ lax.rem(holder + 1, count)
        leads = own_dir ^ lax.rem(holder + count - 1, count)
        ends = dot(tails[follows].astype(BF), head, NN) + dot(tails[leads].astype(BF), tail, NN)
        here = tails[j][:, :dirs]
        spot = count_of((points, LANES), 1)
        spot = jnp.where(spot < rim, spot + dirs, spot - 2 * rim)
        spots = [here[:points].astype(I32) + count_of((points, dirs), 1)]
        spots.append(ends[:points].astype(I32) + spot)
        gains = [here[points:], ends[points:]]
        start = holder * dirs
        after = receive_ref[pl.ds(lax.rem(start + dirs, total), rim)]
        before = receive_ref[pl.ds(lax.rem(start + total - rim, total), rim)]
        tables = [receive_ref[pl.ds(start, dirs)], jnp.concatenate([after, before], axis=0)]
        folded = None
        for spot, gain, table in zip(spots, gains, tables):
            extent = spot.shape[1]
            own = count_of((dirs, extent), 0)
            spread = jnp.zeros((dirs, extent), F32)
            for p in range(points):
                spread += jnp.where(own == spot[p : p + 1, :], gain[p : p + 1, :], 0.0)
            flat = jnp.concatenate([table[:, 0, :], table[:, 1, :]], axis=1)
            if flat.shape[0] < extent:
                blank = jnp.zeros((extent - flat.shape[0], flat.shape[1]), BF)
                flat = jnp.concatenate([flat, blank], axis=0)
            part = dot(spread.astype(BF), flat, NN)
            folded = part if folded is None else folded + part
        folded_ref[at * dirs : (at + 1) * dirs, :] = folded.astype(BF)


def own_pattern(place, forward, receiving, shards, slots, incid, points):
    count = len(shards)
    boxes = sum(s.shape[0] // incid for s in shards)
    rows, width = forward.shape
    out_shape = (
        jax.ShapeDtypeStruct((rows, boxes, 2 * incid), BF),
        jax.ShapeDtypeStruct((rows, width), BF),
    )
    scratch = [
        pltpu.VMEM((padded_rows(rows, boxes), 2 * incid), F32),
        pltpu.VMEM((count, 2 * points, shards[0].shape[1]), F32),
    ]
    return pl.pallas_call(
        functools.partial(pattern_kernel, slots, count, incid, RIM),
        out_shape=out_shape,
        in_specs=[SMEM] + [VMEM] * (2 + count),
        out_specs=(VMEM, VMEM),
        scratch_shapes=scratch,
        compiler_params=grant(scratch, out_shape, shards, [forward, receiving]),
        cost_estimate=cost(4 << 30, 4 << 20),
        name="pattern",
    )(place, forward, receiving, *shards)


def receive(moved, folded, first, out_ref, stride):
    rows, half, unk = folded.shape[0], moved.shape[1] // 2, folded.shape[1] // 2
    count = out_ref.shape[0]
    step = 4 if count % 4 == 0 else 1
    for begin in range(0, count, step):
        fields = [
            moved[pl.ds(first + begin + i, rows, stride=stride), :].astype(BF) for i in range(step)
        ]
        every = dot(jnp.concatenate(fields, axis=1), folded[...], TN)
        for i in range(step):
            full = every[2 * half * i : 2 * half * (i + 1)]
            re = full[:half, :unk] - full[half:, unk:]
            im = full[:half, unk:] + full[half:, :unk]
            out_ref[begin + i] = jnp.concatenate([re, im], axis=1).astype(out_ref.dtype)


def translate(part, matrix_refs, own_ref, early_ref, near, moved):
    rows, own_boxes, width = own_ref.shape
    dirs, lines, _ = matrix_refs[0].shape
    per, half = lines // 4, width // 2
    near_boxes = near.shape[0] // rows - 1
    window = own_boxes + early_ref.shape[1] + near_boxes
    sign = jnp.where(count_of((per, width), 1) < half, -1.0, 1.0).astype(F32)
    for at, matrix_ref in enumerate(matrix_refs):

        def two(i, at=at, matrix_ref=matrix_ref):
            fields, weights = [], []
            for j in (2 * i, 2 * i + 1):
                k = at * dirs + j
                around = near[pl.ds(k * (near_boxes + 1), near_boxes), :].astype(BF)
                fields.append(jnp.concatenate([own_ref[k], early_ref[k], around], axis=0))
                weights.append(matrix_ref[j][2 * per * part : 2 * per * (part + 1), :window])
            both = dot(jnp.concatenate(weights, axis=0), jnp.concatenate(fields, axis=1), NN)
            for j in range(2):
                each = both[2 * per * j : 2 * per * (j + 1), width * j : width * (j + 1)]
                turned = pltpu.roll(each[per:], half, 1)
                begin = (at * dirs + 2 * i + j) * (per + 1)
                moved[pl.ds(begin, per), :] = each[:per] + sign * turned

        unrolled(dirs // 2, 32, two)


def field_kernel(slices, forward_ref, folded_ref, own_ref, early_ref, *refs):
    matrix_refs, refs = refs[:slices], refs[slices:]
    box_refs, (pair_ref, near, moved) = refs[:-3], refs[-3:]
    per, half, _ = pair_ref.shape
    radiate(forward_ref, box_refs, half, near, len(box_refs) * per + 1)
    translate(1, matrix_refs, own_ref, early_ref, near, moved)
    receive(moved, folded_ref, 0, pair_ref, per + 1)


def translate_field(forward, folded, own, early, matrices, near, kind):
    rows, _, width = own.shape
    per = matrices[0].shape[1] // 4
    shape = (per, width // 2, folded.shape[1])
    out_shape = (
        jax.ShapeDtypeStruct(shape, kind),
        jax.ShapeDtypeStruct((padded_rows(rows, len(near) * per), width), F32),
    )
    scratch = [pltpu.VMEM((padded_rows(rows, per), width), F32)]
    return pl.pallas_call(
        functools.partial(field_kernel, len(matrices)),
        out_shape=out_shape,
        in_specs=[VMEM] * (4 + len(matrices) + len(near)),
        out_specs=(VMEM, VMEM),
        scratch_shapes=scratch,
        compiler_params=grant(scratch, out_shape, [forward, folded, own, early], matrices, near),
        cost_estimate=cost(4 << 30, 16 << 20),
        name="field",
    )(forward, folded, own, early, *matrices, *near)


def finish_kernel(slices, folded_ref, own_ref, early_ref, near_ref, *refs):
    matrix_refs, (out_ref, moved) = refs[:slices], refs[slices:]
    translate(0, matrix_refs, own_ref, early_ref, near_ref, moved)
    receive(moved, folded_ref, 0, out_ref, out_ref.shape[0] + 1)


def finish(folded, own, early, around, matrices, shape):
    out_shape = jax.ShapeDtypeStruct(shape, F32)
    rows, _, width = own.shape
    scratch = [pltpu.VMEM((padded_rows(rows, shape[0]), width), F32)]
    return pl.pallas_call(
        functools.partial(finish_kernel, len(matrices)),
        out_shape=out_shape,
        in_specs=[VMEM] * (4 + len(matrices)),
        out_specs=VMEM,
        scratch_shapes=scratch,
        compiler_params=grant(scratch, [out_shape, folded, own, early, around], matrices),
        cost_estimate=cost(2 << 30, 8 << 20),
        name="finish",
    )(folded, own, early, around, *matrices)


def mask_rows(values, live_counts):
    column = jnp.arange(values.shape[-1], dtype=I32) % (values.shape[-1] // 2)
    keep = column[None, None, :] < live_counts[:, None, None]
    return jnp.where(keep, values, jnp.zeros_like(values))


def body(
    currents,
    live_counts,
    radiation,
    sources,
    operator_ids,
    translators,
    stencil,
    stencil_weights,
    receiving,
):
    n_dir, n_grp = lax.axis_size("dir"), lax.axis_size("grp")
    _, _, dirs = translators.shape
    per, incid, _ = currents.shape
    points = stencil.shape[1]
    window = round_up((2 * n_dir + 2) * per, LANES)
    place = jnp.stack([lax.axis_index("dir"), lax.axis_index("grp")]).astype(I32)

    def swap(values, bit):
        return lax.ppermute(values, "dir", [(i, i ^ bit) for i in range(n_dir)])

    def gather(values, last):
        slots = {0: values}
        bit = n_dir // 2
        while bit >= last:
            for j in sorted(slots):
                slots[j + bit] = swap(slots[j], bit)
            bit //= 2
        return [slots[j] for j in sorted(slots)]

    def across(values, step_of):
        pairs = []
        for g in range(n_grp):
            for d in range(n_dir):
                to = g + step_of(d, g)
                if 0 <= to < n_grp:
                    pairs.append((g * n_dir + d, to * n_dir + d))
        return lax.ppermute(values, ("grp", "dir"), pairs)

    shard = prepare(
        live_counts, stencil.T, stencil_weights.T, currents, radiation.shape[0]
    )
    shards = gather(shard, 1)
    near = [across(shards[j], lambda d, g, j=j: 1 if d ^ j > d else -1) for j in range(2, n_dir)]
    next_to = []
    for j in range(2):
        next_to.append(across(shards[j], lambda d, g: 1 if g % 2 else -1))
        next_to.append(across(shards[j], lambda d, g: -1 if g % 2 else 1))
    counts, matrix, part = first_transfer(place, sources, operator_ids, translators, n_dir, window)
    matrices = [matrix]
    for j, mine in enumerate(gather(part, 2)[1:], 1):
        other = across(mine, lambda d, g: -1 if g % 2 else 1)
        matrices.append(transfer(place, counts, mine, other, 2 * per, window))
    bulk = dirs * ((n_dir + 4) * per + 1) * LANES * 4
    slices = len(matrices)
    size = max(n for n in range(1, slices + 1) if slices % n == 0 and (n == 1 or n * bulk <= 20 << 20))
    sums = None
    for first in range(0, slices, size):
        slots = [2 * j for j in range(first, first + size)]
        early, forward = early_pattern(place, radiation, next_to, slots, incid, dirs)
        own, folded = own_pattern(place, forward, receiving, shards, slots, incid, points)
        kind = BF if size == slices else F32
        pair, around = translate_field(
            forward, folded, own, early, matrices[first : first + size], near, kind
        )
        mine = finish(
            folded, own, early, around, matrices[first : first + size], pair.shape
        )
        product = [mine, pair]
        sums = product if sums is None else [a + b for a, b in zip(sums, product)]
    total = sums[0] + swap(sums[1].astype(BF), 1).astype(F32)
    return mask_rows(total, live_counts)


def solution(mesh):
    placed = (
        P(("grp", "dir"), None, None),
        P(("grp", "dir")),
        P(),
        P("grp", None),
        P("grp", None),
        P(None, None, "dir"),
        P("dir", None),
        P("dir", None),
        P(),
    )
    return jax.shard_map(
        body,
        mesh=mesh,
        in_specs=placed,
        out_specs=P(("grp", "dir"), None, None),
        check_vma=False,
    )
```
